512 devices in a mesh: fsdp: 32 (over y_lo, z), expert: 16 (over x, y_hi, core).
Axes of the slice: x: 4, y: 4 (y_hi: 2, y_lo: 2; y = y_hi * 2 + y_lo), z: 16, core: 2. Of those that a mesh axis runs over, the one named last changes fastest.
Arguments:
- tokens: bfloat16 [131072, 1440], P(('fsdp', 'expert')), may hold values from -6 to 6
- cotangent: bfloat16 [131072, 1440], P(('fsdp', 'expert')), may hold values from -6 to 6
- expert_ids: int32 [131072, 4], P(('fsdp', 'expert')), may hold values from 0 to 127, as said below
- gates: float32 [131072, 4], P(('fsdp', 'expert')), may hold values from 0.1 to 0.6
- gate_up_weight: bfloat16 [16, 1440, 2880], P('expert', 'fsdp'), may hold values from -0.15625 to 0.15625
- down_matrix: bfloat16 [16, 1440, 1440], P('expert', 'fsdp'), may hold values from -0.15625 to 0.15625
Outputs:
- output: bfloat16 [131072, 1440], P(('fsdp', 'expert'))
- input_grad: bfloat16 [131072, 1440], P(('fsdp', 'expert'))
The draws below stay inside these ranges and needn't reach their ends.
Inputs may be any that keep to these rules, and one draw needn't show every extreme that they name: `expert_ids`: each row names 4 different experts.
All inputs are finite; a program needn't handle non-finite values.
Results may differ from the reference program's by a relative error of at most 0.006.
Values may be sent and summed in bfloat16 or wider, within the bound.
A program may use at most 128 MiB of HBM per device.

```python
import jax
import jax.numpy as jnp
from jax import lax

D = 1440
FF = 1440
ROUTED_EXPERTS = 128
TOP = 4
TOK_DEV = 256
CAP = 16
WINDOW = 16
TOKENS = 131072
N_FSDP = 32


def draw_expert_ids(key, part):
    key_favored, key_score = jax.random.split(jax.random.fold_in(key, 11))
    favored_expert = jax.random.randint(key_favored, (), 0, WINDOW)
    baseline_logit = jax.random.randint(key_score, (TOKENS, ROUTED_EXPERTS), 0, 65536)
    extra_logit = jnp.where(jnp.arange(ROUTED_EXPERTS) == favored_expert, 12000, 0)
    router_score = (baseline_logit + extra_logit[None, :]) * ROUTED_EXPERTS + jnp.arange(ROUTED_EXPERTS)[None, :]
    values, chosen = lax.top_k(router_score, TOP)
    return chosen.astype(jnp.int32)


def shard_levels(stream_key, dims, shards, low, high):
    gain = 1.0
    for dim, parts in shards:
        draws = jax.random.uniform(jax.random.fold_in(jax.random.fold_in(stream_key, 6), dim), (parts,), jnp.float32, low / len(shards), high / len(shards))
        gain = gain * jnp.repeat(jnp.exp(draws), dims[dim] // parts).reshape((-1,) + (1,) * (len(dims) - 1 - dim))
    return gain


def noise(rng, dims, scale, most, cuts=(), kind=jnp.bfloat16):
    loudness = shard_levels(rng, dims, cuts, -0.22, 0.18) if cuts else 1.0
    values = jax.random.normal(rng, dims, jnp.float32) * scale * loudness
    return jnp.minimum(jnp.maximum(values, -most), most).astype(kind)


def setup_inputs(seed: int = 0) -> dict:
    splits = jax.random.split(jax.random.key(seed), 7)
    return {
        "tokens": noise(splits[0], (TOKENS, D), 1.0, 6.0, ((0, 512),)),
        "cotangent": noise(splits[1], (TOKENS, D), 1.0, 6.0, ((0, 512),)),
        "expert_ids": draw_expert_ids(jax.random.fold_in(splits[6], 71), 0),
        "gates": jnp.clip(0.1 + 0.5 * jax.random.uniform(splits[3], (TOKENS, TOP), jnp.float32) ** shard_levels(splits[3], (TOKENS, TOP), ((0, 512),), -0.2, 0.2), 0.1, 0.6),
        "gate_up_weight": noise(splits[4], (WINDOW, D, 2 * FF), D ** -0.5, 0.15625, ((0, 16), (1, 32))),
        "down_matrix": noise(splits[5], (WINDOW, FF, D), FF ** -0.5, 0.15625, ((0, 16), (1, 32))),
    }


def slot_places(expert_ids, window, slot_capacity):
    count = expert_ids.shape[0]
    choose = expert_ids.shape[1]
    flat = expert_ids.reshape(-1)
    onehot = (flat[:, None] == jnp.arange(window, dtype=jnp.int32)[None, :]).astype(jnp.int32)
    before = jnp.cumsum(onehot, axis=0) - onehot
    slot = jnp.sum(before * onehot, axis=1).astype(jnp.int32)
    kept = (flat < window) & (slot < slot_capacity)
    places = jnp.where(kept, flat * slot_capacity + slot, window * slot_capacity)
    return places.astype(jnp.int32).reshape(count, choose)


def expert_pass(rows, grad_rows, gate_up_matrix, down):
    width = down.shape[0]
    pre = jnp.dot(rows, gate_up_matrix, preferred_element_type=jnp.float32)
    act = pre[:, :width]
    upper = pre[:, width:]
    sigma = jax.nn.sigmoid(act)
    hidden = (act * sigma * upper).astype(jnp.bfloat16)
    result = jnp.dot(hidden, down, preferred_element_type=jnp.float32).astype(jnp.bfloat16)
    hidden_grad = jnp.dot(grad_rows, down.T, preferred_element_type=jnp.float32)
    pre_grad = jnp.concatenate([hidden_grad * upper * sigma * (1.0 + act * (1.0 - sigma)), hidden_grad * act * sigma], axis=1).astype(jnp.bfloat16)
    back = jnp.dot(pre_grad, gate_up_matrix.T, preferred_element_type=jnp.float32).astype(jnp.bfloat16)
    return result, back


def block_buffers(rows, grads, expert_ids, gates):
    places = slot_places(expert_ids, WINDOW, CAP).reshape(-1)
    many = jnp.repeat(rows, TOP, axis=0)
    weighted = gates.reshape(-1)[:, None] * jnp.repeat(grads, TOP, axis=0).astype(jnp.float32)
    send_rows = jnp.zeros((WINDOW * CAP + 1, D), jnp.bfloat16).at[places].set(many)[:-1]
    send_grads = jnp.zeros((WINDOW * CAP + 1, D), jnp.float32).at[places].set(weighted)[:-1].astype(jnp.bfloat16)
    return send_rows, send_grads


def block_combine(result, back, expert_ids, gates):
    places = slot_places(expert_ids, WINDOW, CAP)
    pad_result = jnp.concatenate([result, jnp.zeros((1, D), result.dtype)], axis=0)
    pad_back = jnp.concatenate([back, jnp.zeros((1, D), back.dtype)], axis=0)
    out_rows = pad_result[places].astype(jnp.float32)
    back_rows = pad_back[places].astype(jnp.float32)
    output = jnp.sum(gates[:, :, None] * out_rows, axis=1).astype(jnp.bfloat16)
    input_grad = jnp.sum(back_rows, axis=1).astype(jnp.bfloat16)
    return output, input_grad


def swap_blocks(array):
    return array.reshape(WINDOW, WINDOW, CAP, D).transpose(1, 0, 2, 3).reshape(WINDOW, WINDOW * CAP, D)


def reference(tokens, cotangent, expert_ids, gates, gate_up_weight, down_matrix):
    def group(items):
        rows, grads, ids, mixing = items
        send_rows, send_grads = jax.vmap(block_buffers)(rows, grads, ids, mixing)
        at_experts = swap_blocks(send_rows)
        grad_experts = swap_blocks(send_grads)
        result, back = lax.map(lambda a: expert_pass(a[0], a[1], a[2], a[3]), (at_experts, grad_experts, gate_up_weight, down_matrix))
        return jax.vmap(block_combine)(swap_blocks(result), swap_blocks(back), ids, mixing)

    shaped = (tokens.reshape(N_FSDP, WINDOW, TOK_DEV, D), cotangent.reshape(N_FSDP, WINDOW, TOK_DEV, D), expert_ids.reshape(N_FSDP, WINDOW, TOK_DEV, TOP), gates.reshape(N_FSDP, WINDOW, TOK_DEV, TOP))
    output, input_grad = lax.map(group, shaped)
    return output.reshape(TOKENS, D), input_grad.reshape(TOKENS, D)
```

```python
import functools

import jax
import jax.numpy as jnp
import numpy as np
from jax import lax
from jax.experimental import pallas as pl
from jax.experimental.pallas import tpu as pltpu
from jax.sharding import PartitionSpec as P

MESH = pl.DeviceIdType.MESH
CAP = 16
LANE = 128
BF = jnp.bfloat16
F32 = jnp.float32
NN = (((1,), (0,)), ((), ()))
NT = (((1,), (1,)), ((), ()))


def dot(a, b, dims=NN):
    return lax.dot_general(a, b, dims, preferred_element_type=F32)


def onehot(mask):
    return jnp.where(mask, 1.0, 0.0).astype(BF)


def layer_kernel(
    cfg,
    gate_up_hbm, down_hbm, tok_hbm, cot_hbm, ids_ref, gates_ref, place_ref,
    out_ref, igrad_ref,
    gu_own, dn_own, own32, own_gu, own_dn,
    w_gate, w_up, w_down,
    tok, cot, rows_nat, rows_send, rows_in, grads_send, grads_in,
    hid, fac_gate, fac_up, pg_gate, pg_up,
    out_send, rg_send, out_recv, rg_recv,
    pick, pick_t, mix_hi, mix_lo,
    in_sem, swap_send, swap_recv, ring_send_sem, ring_recv_sem, last_send_sem, last_recv_sem,
    sib_send_sem, sib_recv_sem, a2a_send_sem, a2a_recv_sem,
):
    nz, ne, per, pad, width = cfg["nz"], cfg["ne"], cfg["per"], cfg["pad"], cfg["width"]
    dp = 2 * nz * pad
    chunks = w_down.shape[0]
    cw = w_down.shape[2]
    tile = cfg["tile"]
    rows = ne * CAP
    toks = ids_ref.shape[1]
    kb = nz // 2 - 1

    f = lax.axis_index("fsdp")
    e = lax.axis_index("expert")
    ylo = lax.div(f, nz)
    z = lax.rem(f, nz)
    c = lax.rem(e, 2)
    e2 = lax.div(e, 2)
    keeps = ylo == c
    swaps = ylo != c

    barrier = pltpu.get_barrier_semaphore()

    def greet(i, _):
        gf = lax.div(i, ne) * nz + z
        ge = lax.rem(i, ne)

        @pl.when((gf != f) | (ge != e))
        def _():
            pl.semaphore_signal(barrier, inc=1, device_id=(gf, ge), device_id_type=MESH)

        return 0

    znext = ylo * nz + lax.rem(z + 1, nz)
    zprev = ylo * nz + lax.rem(z + nz - 1, nz)
    pl.semaphore_signal(barrier, inc=1, device_id=(znext, e), device_id_type=MESH)
    pl.semaphore_signal(barrier, inc=1, device_id=(zprev, e), device_id_type=MESH)
    lax.fori_loop(0, 2 * ne, greet, 0)

    load_gu = pltpu.make_async_copy(gate_up_hbm, gu_own, in_sem.at[0])
    load_dn = pltpu.make_async_copy(down_hbm, dn_own, in_sem.at[1])
    load_tok = pltpu.make_async_copy(tok_hbm, tok.at[pl.ds(0, width)], in_sem.at[2])
    load_cot = pltpu.make_async_copy(cot_hbm, cot.at[pl.ds(0, width)], in_sem.at[3])
    load_gu.start()
    load_dn.start()
    load_tok.start()
    load_cot.start()

    def spans(base, j):
        p = np.arange(LANE * j, LANE * (j + 1))
        p = p[p % pad < per]
        d = per * (p // pad) + p % pad + base
        start = int(d.min()) // LANE * LANE
        assert d.max() < start + 2 * LANE
        return start

    own32[...] = jnp.zeros_like(own32)
    load_gu.wait()
    for half in range(2):
        for j in range(dp // LANE):
            start = spans(half * width, j)
            depth = min(2 * LANE, 2 * width - start)
            hid_id = lax.broadcasted_iota(jnp.int32, (depth, LANE), 0) + (start - half * width)
            sel = onehot(hid_id == place_ref[0:1, LANE * j : LANE * (j + 1)])
            own32[0:per, LANE * j : LANE * (j + 1)] = dot(gu_own[:, start : start + depth], sel)
        own_gu[half] = own32[...].astype(BF)
    load_dn.wait()
    own32[...] = jnp.zeros_like(own32)
    own32[0:per, 0:width] = dn_own[...].astype(F32)
    for n in range(chunks):
        own_dn[n] = own32[:, cw * n : cw * (n + 1)].astype(BF)

    weights = [w_gate, w_up] + [w_down.at[n] for n in range(chunks)]
    owns = [own_gu.at[0], own_gu.at[1]] + [own_dn.at[n] for n in range(chunks)]

    def block(p, core, b):
        return weights[p].at[pl.ds(pl.multiple_of((core * nz + b) * pad, 16), pad)]

    def wait_for(ref, sem):
        pltpu.make_async_copy(ref, ref, sem).wait()

    def start_swap(p):
        @pl.when(keeps)
        def _():
            pltpu.make_async_copy(owns[p], block(p, c, z), swap_recv.at[p]).start()

        @pl.when(swaps)
        def _():
            pltpu.make_async_remote_copy(
                src_ref=owns[p], dst_ref=block(p, 1 - c, z),
                send_sem=swap_send.at[p], recv_sem=swap_recv.at[p],
                device_id=((1 - ylo) * nz + z, e2 * 2 + 1 - c), device_id_type=MESH,
            ).start()

    def ring_send(p, way, k):
        b = lax.rem(z + nz - k, nz) if way == 0 else lax.rem(z + k, nz)
        pltpu.make_async_remote_copy(
            src_ref=block(p, c, b), dst_ref=block(p, c, b),
            send_sem=ring_send_sem.at[p, way], recv_sem=ring_recv_sem.at[p, way, k],
            device_id=(znext if way == 0 else zprev, e), device_id_type=MESH,
        ).start()

    def last_send(p):
        b = lax.rem(z + nz - (1 - 2 * c) * kb, nz)
        pltpu.make_async_remote_copy(
            src_ref=block(p, c, b), dst_ref=block(p, c, b),
            send_sem=last_send_sem.at[p], recv_sem=last_recv_sem.at[p],
            device_id=(ylo * nz + lax.rem(z + nz + 1 - 2 * c, nz), e), device_id_type=MESH,
        ).start()

    def sib_send(p, b):
        pltpu.make_async_remote_copy(
            src_ref=block(p, c, b), dst_ref=block(p, c, b),
            send_sem=sib_send_sem.at[p], recv_sem=sib_recv_sem.at[p],
            device_id=(f, e2 * 2 + 1 - c), device_id_type=MESH,
        ).start()

    def ring_open(p):
        wait_for(block(p, c, z), swap_recv.at[p])
        ring_send(p, 0, 0)
        ring_send(p, 1, 0)
        sib_send(p, z)

    def ring_step(p, k):
        came = (lax.rem(z + nz - 1 - k, nz), lax.rem(z + 1 + k, nz))
        for way in range(2):
            wait_for(block(p, c, came[way]), ring_recv_sem.at[p, way, k])
            if k < kb - 1:
                ring_send(p, way, k + 1)
            sib_send(p, came[way])
        if k == kb - 1:
            last_send(p)

    def ring_close(p):
        b = lax.rem(z + nz // 2, nz)
        wait_for(block(p, c, b), last_recv_sem.at[p])
        sib_send(p, b)

    def ring_here(p):
        wait_for(weights[p].at[pl.ds(pl.multiple_of((1 - c) * nz * pad, 16), nz * pad)], sib_recv_sem.at[p])

    def go(i, src, dst, gf, ge, place):
        @pl.when((gf != f) | (ge != e))
        def _():
            pltpu.make_async_remote_copy(
                src_ref=src, dst_ref=dst, send_sem=a2a_send_sem.at[i], recv_sem=a2a_recv_sem.at[i],
                device_id=(gf, ge), device_id_type=MESH,
            ).start()

        @pl.when((gf == f) & (ge == e))
        def _():
            pltpu.make_async_copy(src, dst, a2a_recv_sem.at[i]).start()

    def sixteen(ref, i):
        return ref.at[pl.ds(pl.multiple_of(i * CAP, CAP), CAP)]

    def send_out(i, src, dst):
        def one(t, _):
            x = lax.rem(e + t, ne)
            go(i, sixteen(src, x), sixteen(dst, e), lax.rem(x, 2) * nz + z, lax.div(x, 2) * 2 + ylo, x)
            return 0

        lax.fori_loop(0, ne, one, 0)

    def send_back(i, src, dst):
        def one(t, _):
            x = lax.rem(e + t, ne)
            go(i, sixteen(src, x), sixteen(dst, e2 * 2 + ylo), c * nz + z, x, x)
            return 0

        lax.fori_loop(0, ne, one, 0)

    def sent(i, src):
        @pl.when(keeps)
        def _():
            wait_for(src.at[pl.ds(0, rows - CAP)], a2a_send_sem.at[i])

        @pl.when(swaps)
        def _():
            wait_for(src, a2a_send_sem.at[i])

    def make_slots():
        ci = lax.broadcasted_iota(jnp.int32, (rows, toks), 0)
        expert = lax.shift_right_logical(ci, 4)
        hit = jnp.zeros((rows, toks), F32)
        gate = jnp.zeros((rows, toks), F32)
        for k in range(ids_ref.shape[0]):
            same = ids_ref[k : k + 1, :] == expert
            hit = jnp.where(same, 1.0, hit)
            gate = jnp.where(same, gates_ref[k : k + 1, :], gate)
        earlier = onehot(
            lax.broadcasted_iota(jnp.int32, (toks, toks), 0) < lax.broadcasted_iota(jnp.int32, (toks, toks), 1)
        )
        slot = dot(hit.astype(BF), earlier)
        want = jnp.bitwise_and(ci, CAP - 1).astype(F32)
        kept = jnp.where(slot == want, hit, 0.0)
        gate = gate * kept
        pick[...] = kept.astype(BF)
        pick_t[...] = kept.T.astype(BF)
        mixed = gate.T
        high = mixed.astype(BF)
        mix_hi[...] = high
        mix_lo[...] = (mixed - high.astype(F32)).astype(BF)
        return jnp.sum(gate, axis=1, keepdims=True)

    def columns(n):
        return slice(tile * n, tile * (n + 1))

    def make_rows():
        load_tok.wait()
        for n in range(dp // tile):
            rows_nat[:, columns(n)] = dot(pick[...], tok[columns(n), :], NT).astype(BF)
        for j in range(dp // LANE):
            start = spans(0, j)
            depth = min(2 * LANE, dp - start)
            d = lax.broadcasted_iota(jnp.int32, (depth, LANE), 0) + start
            sel = onehot(d == place_ref[0:1, LANE * j : LANE * (j + 1)])
            rows_send[:, LANE * j : LANE * (j + 1)] = dot(rows_nat[:, start : start + depth], sel).astype(BF)

    def make_grads(slot_gate):
        load_cot.wait()
        for n in range(dp // tile):
            grads_send[:, columns(n)] = (dot(pick[...], cot[columns(n), :], NT) * slot_gate).astype(BF)

    def forward_tile(n):
        act = dot(rows_in[...], w_gate[:, columns(n)])
        upper = dot(rows_in[...], w_up[:, columns(n)])
        sigma = jax.nn.sigmoid(act)
        gated = act * sigma
        hid[:, columns(n)] = (gated * upper).astype(BF)
        fac_gate[:, columns(n)] = upper * sigma * (1.0 + act * (1.0 - sigma))
        fac_up[:, columns(n)] = gated

    def backward_tile(n):
        grad = dot(grads_in[:, 0:cw], w_down[0, columns(n), :], NT)
        for m in range(1, chunks):
            grad = grad + dot(grads_in[:, cw * m : cw * (m + 1)], w_down[m, columns(n), :], NT)
        pg_gate[:, columns(n)] = (grad * fac_gate[:, columns(n)]).astype(BF)
        pg_up[:, columns(n)] = (grad * fac_up[:, columns(n)]).astype(BF)

    tok[width:dp, :] = jnp.zeros((dp - width, toks), BF)
    cot[width:dp, :] = jnp.zeros((dp - width, toks), BF)

    pl.semaphore_wait(barrier, 2 * ne + 1)

    first, second = [0, 1], list(range(2, 2 + chunks))
    for p in first + second:
        start_swap(p)
    for p in first:
        ring_open(p)
    slot_gate = make_slots()
    make_rows()
    send_out(0, rows_send, rows_in)
    for p in first:
        ring_step(p, 0)
    make_grads(slot_gate)
    send_out(1, grads_send, grads_in)
    for k in range(1, kb):
        for p in first:
            ring_step(p, k)
    for p in second:
        ring_open(p)
    for p in first:
        ring_close(p)
    for p in first:
        ring_here(p)
    wait_for(rows_in, a2a_recv_sem.at[0])
    tiles = dp // tile
    done = 0
    for k in range(kb):
        for p in second:
            ring_step(p, k)
        upto = tiles if k == kb - 1 else min(tiles, k + 1)
        for n in range(done, upto):
            forward_tile(n)
        done = upto
    for p in second:
        ring_close(p)
    wait_for(grads_in, a2a_recv_sem.at[1])
    for n in range(chunks):
        ring_here(2 + n)
        out_send[n] = dot(hid[...], w_down[n]).astype(BF)
        send_back(2 + n, out_send.at[n], out_recv.at[n])
    for n in range(tiles):
        backward_tile(n)
    for n in range(chunks):
        for m in range(cw // tile):
            here = slice(cw * n + tile * m, cw * n + tile * (m + 1))
            rg_send[n, :, columns(m)] = (
                dot(pg_gate[...], w_gate[here, :], NT) + dot(pg_up[...], w_up[here, :], NT)
            ).astype(BF)
        send_back(2 + chunks + n, rg_send.at[n], rg_recv.at[n])

    eye = onehot(
        lax.broadcasted_iota(jnp.int32, (LANE, LANE), 0) == lax.broadcasted_iota(jnp.int32, (LANE, LANE), 1)
    )
    for n in range(chunks):
        wait_for(out_recv.at[n], a2a_recv_sem.at[2 + n])
        total = (dot(mix_hi[...], out_recv[n]) + dot(mix_lo[...], out_recv[n])).astype(BF)
        for m in range(cw // LANE):
            d = cw * n + LANE * m
            size = min(LANE, width - d)
            if size > 0:
                turned = dot(eye, total[:, LANE * m : LANE * (m + 1)], NT).astype(BF)
                out_ref[d : d + size, :] = turned[0:size, :]
    for n in range(chunks):
        wait_for(rg_recv.at[n], a2a_recv_sem.at[2 + chunks + n])
        rows_nat[:, cw * n : cw * (n + 1)] = dot(pick_t[...], rg_recv[n]).astype(BF)
    for j in range(pl.cdiv(width, LANE)):
        d = np.arange(LANE * j, min(width, LANE * (j + 1)))
        p = pad * (d // per) + d % per
        start = int(p.min()) // LANE * LANE
        stop = (int(p.max()) // LANE + 1) * LANE
        di = lax.broadcasted_iota(jnp.int32, (LANE, stop - start), 0) + LANE * j
        sel = onehot(di == place_ref[0:1, start:stop])
        turned = dot(sel, rows_nat[:, start:stop], NT).astype(BF)
        igrad_ref[LANE * j : LANE * j + len(d), :] = turned[0 : len(d), :]

    for p in first + second:
        for way in range(2):
            wait_for(weights[p].at[pl.ds(0, kb * pad)], ring_send_sem.at[p, way])
        wait_for(weights[p].at[pl.ds(0, pad)], last_send_sem.at[p])
        wait_for(weights[p].at[pl.ds(0, nz * pad)], sib_send_sem.at[p])

        @pl.when(swaps)
        def _():
            wait_for(owns[p], swap_send.at[p])

    sent(0, rows_send)
    sent(1, grads_send)
    for n in range(chunks):
        sent(2 + n, out_send.at[n])
        sent(2 + chunks + n, rg_send.at[n])


def shards(mesh_shape, tokens, cotangent, expert_ids, gates, gate_up_weight, down_matrix):
    ne = mesh_shape["expert"]
    nz = mesh_shape["fsdp"] // 2
    toks, width = tokens.shape
    per = down_matrix.shape[1]
    pad = pl.cdiv(per, 16) * 16
    dp = 2 * nz * pad
    chunks = 3
    cw = dp // chunks
    tile = 256 if cw % 256 == 0 else 128
    rows = ne * CAP
    pieces = 2 + chunks
    p = np.arange(dp)
    place = np.where(p % pad < per, per * (p // pad) + p % pad, -(1 << 20)).astype(np.int32)[None]
    cfg = dict(nz=nz, ne=ne, per=per, pad=pad, width=width, tile=tile)
    any_spec = pl.BlockSpec(memory_space=pl.ANY)
    vmem_spec = pl.BlockSpec(memory_space=pltpu.VMEM)
    dma = pltpu.SemaphoreType.DMA
    flat = (rows, dp)
    out_t, grad_t = pl.pallas_call(
        functools.partial(layer_kernel, cfg),
        out_shape=[jax.ShapeDtypeStruct((width, toks), BF)] * 2,
        in_specs=[any_spec] * 4 + [vmem_spec] * 3,
        out_specs=[vmem_spec] * 2,
        scratch_shapes=[
            pltpu.VMEM((per, 2 * width), BF),
            pltpu.VMEM((per, width), BF),
            pltpu.VMEM((pad, dp), F32),
            pltpu.VMEM((2, pad, dp), BF),
            pltpu.VMEM((chunks, pad, cw), BF),
            pltpu.VMEM((dp, dp), BF),
            pltpu.VMEM((dp, dp), BF),
            pltpu.VMEM((chunks, dp, cw), BF),
            pltpu.VMEM((dp, toks), BF),
            pltpu.VMEM((dp, toks), BF),
            pltpu.VMEM((toks, dp), BF),
            pltpu.VMEM(flat, BF),
            pltpu.VMEM(flat, BF),
            pltpu.VMEM(flat, BF),
            pltpu.VMEM(flat, BF),
            pltpu.VMEM(flat, BF),
            pltpu.VMEM(flat, F32),
            pltpu.VMEM(flat, F32),
            pltpu.VMEM(flat, BF),
            pltpu.VMEM(flat, BF),
            pltpu.VMEM((chunks, rows, cw), BF),
            pltpu.VMEM((chunks, rows, cw), BF),
            pltpu.VMEM((chunks, rows, cw), BF),
            pltpu.VMEM((chunks, rows, cw), BF),
            pltpu.VMEM((rows, toks), BF),
            pltpu.VMEM((toks, rows), BF),
            pltpu.VMEM((toks, rows), BF),
            pltpu.VMEM((toks, rows), BF),
            dma((4,)),
            dma((pieces,)),
            dma((pieces,)),
            dma((pieces, 2)),
            dma((pieces, 2, nz // 2)),
            dma((pieces,)),
            dma((pieces,)),
            dma((pieces,)),
            dma((pieces,)),
            dma((2 + 2 * chunks,)),
            dma((2 + 2 * chunks,)),
        ],
        compiler_params=pltpu.CompilerParams(
            collective_id=0, has_side_effects=True, vmem_limit_bytes=60 * 1024 * 1024
        ),
    )(gate_up_weight[0], down_matrix[0], tokens.T, cotangent.T, expert_ids.T, gates.T, jnp.asarray(place))
    return out_t.T, grad_t.T


def solution(mesh):
    in_specs = (
        P(("fsdp", "expert"), None),
        P(("fsdp", "expert"), None),
        P(("fsdp", "expert"), None),
        P(("fsdp", "expert"), None),
        P("expert", "fsdp", None),
        P("expert", "fsdp", None),
    )
    out_specs = (P(("fsdp", "expert"), None), P(("fsdp", "expert"), None))
    return jax.shard_map(
        functools.partial(shards, dict(mesh.shape)), mesh=mesh, in_specs=in_specs, out_specs=out_specs, check_vma=False
    )
```

```python
import functools

import jax
import jax.numpy as jnp
import numpy as np
from jax import lax
from jax.experimental import pallas as pl
from jax.experimental.pallas import tpu as pltpu
from jax.sharding import PartitionSpec as P

MESH = pl.DeviceIdType.MESH
CAP = 16
LANE = 128
BF = jnp.bfloat16
F32 = jnp.float32
NN = (((1,), (0,)), ((), ()))
NT = (((1,), (1,)), ((), ()))


def dot(a, b, dims=NN):
    return lax.dot_general(a, b, dims, preferred_element_type=F32)


def onehot(mask):
    return jnp.where(mask, 1.0, 0.0).astype(BF)


def windows(idx, width, cuts):
    edges = [0, *cuts, width]
    found = []
    for lo, hi in zip(edges[:-1], edges[1:]):
        part = idx[(idx >= lo) & (idx < hi)]
        if part.size:
            start = int(part.min()) // LANE * LANE
            found.append((start, min(pl.cdiv(int(part.max()) + 1, LANE) * LANE, hi)))
    return found


def tables(nz, per, pad, width):
    ns = 2 * nz
    dp = ns * pad
    main = per // 8 * 8
    rest = per - main
    head = ns * main
    q = np.arange(width)
    s = np.where(q < head, q // main, (q - head) // rest)
    i = np.where(q < head, q % main, main + (q - head) % rest)
    nat_q, pad_q = per * s + i, pad * s + i
    p = np.arange(dp)
    place = np.where(p % pad < per, per * (p // pad) + p % pad, -1)
    packed_p = np.full(dp, -1)
    packed_p[pad_q] = q
    tail = (width - head) // LANE * LANE
    odd = width - head - tail
    gate_q = np.concatenate([np.arange(head), 2 * head + np.arange(tail), 2 * head + 2 * tail + np.arange(odd)])
    up_q = np.concatenate([head + np.arange(head), 2 * head + tail + np.arange(tail), 2 * head + 2 * tail + odd + np.arange(odd)])
    down_at = 2 * width
    total = pl.cdiv(3 * width, LANE) * LANE
    first = down_at // LANE * LANE
    assert total - first == dp and head % LANE == 0
    own = np.full(total, -1)
    own[gate_q] = nat_q
    own[up_q] = width + nat_q
    from_gate = np.full(total, -1)
    from_gate[gate_q] = pad_q
    from_up = np.full(total, -1)
    from_up[up_q] = pad_q
    table = np.full((8, total), -1, np.int32)
    table[0], table[1, :dp], table[2, :dp], table[3], table[4] = own, place, packed_p, from_gate, from_up
    return dict(head=head, tail=tail, odd=odd, first=first, shift=down_at - first, total=total, dp=dp, table=table)


def layer_kernel(
    cfg,
    gate_up_hbm, down_hbm, tok_hbm, cot_hbm, ids_ref, gates_ref, table_ref,
    out_ref, igrad_ref,
    gu_own, dn_own, own32, own, weights,
    tok, cot, rows_nat, rows_send, rows_in, grads_send, grads_in,
    hid, fac_gate_hi, fac_gate_lo, fac_up_hi, fac_up_lo, hid_pad, fac_gate, fac_up, hid_grad, pg_gate, pg_up, pg,
    out_send, rg_send, out_recv, rg_recv,
    pick, pick_t, mix_hi, mix_lo,
    in_sem, swap_send, swap_recv, ring_send_sem, ring_recv_sem, last_send_sem, last_recv_sem,
    sib_send_sem, sib_recv_sem, a2a_send_sem, a2a_recv_sem, round_sem,
):
    nz, ne, per, pad, width = cfg["nz"], cfg["ne"], cfg["per"], cfg["pad"], cfg["width"]
    head, tail, odd, first, shift = cfg["head"], cfg["tail"], cfg["odd"], cfg["first"], cfg["shift"]
    dp, total, table, pieces = cfg["dp"], cfg["total"], cfg["table"], cfg["pieces"]
    chunks, rows, cw = out_send.shape
    tile = cfg["tile"]
    toks = ids_ref.shape[1]
    kb = nz // 2 - 1

    f = lax.axis_index("fsdp")
    e = lax.axis_index("expert")
    ylo = lax.div(f, nz)
    z = lax.rem(f, nz)
    c = lax.rem(e, 2)
    e2 = lax.div(e, 2)
    keeps = ylo == c
    swaps = ylo != c
    znext = ylo * nz + lax.rem(z + 1, nz)
    zprev = ylo * nz + lax.rem(z + nz - 1, nz)

    bits = ne.bit_length() - 1
    partners = [((1 - ylo) * nz + z, e)]
    for r in range(bits):
        bit = lax.rem(lax.div(e, 2**r), 2)
        partners.append((f, e + (1 - 2 * bit) * 2**r))
    swap_partner = ((1 - ylo) * nz + z, e2 * 2 + 1 - c)
    barrier = pltpu.get_barrier_semaphore()
    near = [(znext, e), (zprev, e), swap_partner] + partners
    for there in near:
        pl.semaphore_signal(barrier, inc=1, device_id=there, device_id_type=MESH)

    def round_signal(r):
        pl.semaphore_signal(round_sem.at[r], inc=1, device_id=partners[r], device_id_type=MESH)

    def round_wait(r):
        pl.semaphore_wait(round_sem.at[r], 1)

    load_gu = pltpu.make_async_copy(gate_up_hbm, gu_own, in_sem.at[0])
    load_dn = pltpu.make_async_copy(down_hbm, dn_own, in_sem.at[1])
    load_tok = pltpu.make_async_copy(tok_hbm, tok.at[pl.ds(0, width)], in_sem.at[2])
    load_cot = pltpu.make_async_copy(cot_hbm, cot.at[pl.ds(shift, width)], in_sem.at[3])
    load_gu.start()
    load_dn.start()
    load_tok.start()
    load_cot.start()

    def pick_columns(src, row, j, cuts=()):
        acc = None
        for start, stop in windows(table[row, LANE * j : LANE * (j + 1)], src.shape[1], cuts):
            col = lax.broadcasted_iota(jnp.int32, (stop - start, LANE), 0) + start
            part = dot(src[:, start:stop], onehot(col == table_ref[row : row + 1, LANE * j : LANE * (j + 1)]))
            acc = part if acc is None else acc + part
        return acc

    own32[...] = jnp.zeros_like(own32)
    load_gu.wait()
    load_dn.wait()
    for j in range(total // LANE):
        part = None
        if (table[0, LANE * j : LANE * (j + 1)] >= 0).any():
            part = pick_columns(gu_own, 0, j, (width // LANE * LANE,))
        lo = max(LANE * j - 2 * width, 0)
        hi = min(LANE * (j + 1) - 2 * width, width)
        if hi > 0:
            start, stop = lo // LANE * LANE, min(pl.cdiv(hi, LANE) * LANE, width)
            col = lax.broadcasted_iota(jnp.int32, (stop - start, LANE), 0) + (start + 2 * width)
            lane = lax.broadcasted_iota(jnp.int32, (stop - start, LANE), 1) + LANE * j
            more = dot(dn_own[:, start:stop], onehot(col == lane))
            part = more if part is None else part + more
        own32[0:per, LANE * j : LANE * (j + 1)] = part
    own[...] = own32[...].astype(BF)

    def piece(p, at, size):
        start, wide = pieces[p]
        return weights.at[pl.ds(pl.multiple_of(at, 16), size), pl.ds(start, wide)]

    def own_piece(p):
        start, wide = pieces[p]
        return own.at[:, pl.ds(start, wide)]

    def block(p, core, b):
        return piece(p, (core * nz + b) * pad, pad)

    def wait_for(ref, sem):
        pltpu.make_async_copy(ref, ref, sem).wait()

    def start_swap(p):
        @pl.when(keeps)
        def _():
            pltpu.make_async_copy(own_piece(p), block(p, c, z), swap_recv.at[p]).start()

        @pl.when(swaps)
        def _():
            pltpu.make_async_remote_copy(
                src_ref=own_piece(p), dst_ref=block(p, 1 - c, z),
                send_sem=swap_send.at[p], recv_sem=swap_recv.at[p],
                device_id=swap_partner, device_id_type=MESH,
            ).start()

    def ring_send(p, way, k):
        b = lax.rem(z + nz - k, nz) if way == 0 else lax.rem(z + k, nz)
        pltpu.make_async_remote_copy(
            src_ref=block(p, c, b), dst_ref=block(p, c, b),
            send_sem=ring_send_sem.at[p, way], recv_sem=ring_recv_sem.at[p, way, k],
            device_id=(znext if way == 0 else zprev, e), device_id_type=MESH,
        ).start()

    def last_send(p):
        b = lax.rem(z + nz - (1 - 2 * c) * kb, nz)
        pltpu.make_async_remote_copy(
            src_ref=block(p, c, b), dst_ref=block(p, c, b),
            send_sem=last_send_sem.at[p], recv_sem=last_recv_sem.at[p],
            device_id=(ylo * nz + lax.rem(z + nz + 1 - 2 * c, nz), e), device_id_type=MESH,
        ).start()

    def sib_send(p, b):
        pltpu.make_async_remote_copy(
            src_ref=block(p, c, b), dst_ref=block(p, c, b),
            send_sem=sib_send_sem.at[p], recv_sem=sib_recv_sem.at[p],
            device_id=(f, e2 * 2 + 1 - c), device_id_type=MESH,
        ).start()

    def ring_open(p):
        wait_for(block(p, c, z), swap_recv.at[p])
        ring_send(p, 0, 0)
        ring_send(p, 1, 0)
        sib_send(p, z)

    def ring_step(p, k):
        came = (lax.rem(z + nz - 1 - k, nz), lax.rem(z + 1 + k, nz))
        for way in range(2):
            wait_for(block(p, c, came[way]), ring_recv_sem.at[p, way, k])
            if k < kb - 1:
                ring_send(p, way, k + 1)
            sib_send(p, came[way])
        if k == kb - 1:
            last_send(p)

    def ring_close(p):
        b = lax.rem(z + nz // 2, nz)
        wait_for(block(p, c, b), last_recv_sem.at[p])
        sib_send(p, b)

    def ring_here(p):
        wait_for(piece(p, (1 - c) * nz * pad, nz * pad), sib_recv_sem.at[p])

    def go(i, src, dst, gf, ge):
        @pl.when((gf != f) | (ge != e))
        def _():
            pltpu.make_async_remote_copy(
                src_ref=src, dst_ref=dst, send_sem=a2a_send_sem.at[i], recv_sem=a2a_recv_sem.at[i],
                device_id=(gf, ge), device_id_type=MESH,
            ).start()

        @pl.when((gf == f) & (ge == e))
        def _():
            pltpu.make_async_copy(src, dst, a2a_recv_sem.at[i]).start()

    def sixteen(ref, i):
        return ref.at[pl.ds(pl.multiple_of(i * CAP, CAP), CAP)]

    def send_out(i, src, dst):
        def one(t, _):
            x = lax.rem(e + t, ne)
            go(i, sixteen(src, x), sixteen(dst, e), lax.rem(x, 2) * nz + z, lax.div(x, 2) * 2 + ylo)
            return 0

        lax.fori_loop(0, ne, one, 0)

    def send_back(i, src, dst):
        def one(t, _):
            x = lax.rem(e + ne // 2 + lax.div(t, 2) * (1 - 2 * lax.rem(t, 2)) - lax.rem(t, 2) + ne, ne)
            go(i, sixteen(src, x), sixteen(dst, e2 * 2 + ylo), c * nz + z, x)
            return 0

        lax.fori_loop(0, ne, one, 0)

    def sent(i, src):
        @pl.when(keeps)
        def _():
            wait_for(src.at[pl.ds(0, rows - CAP)], a2a_send_sem.at[i])

        @pl.when(swaps)
        def _():
            wait_for(src, a2a_send_sem.at[i])

    def make_slots():
        ci = lax.broadcasted_iota(jnp.int32, (rows, toks), 0)
        expert = lax.shift_right_logical(ci, 4)
        hit = jnp.zeros((rows, toks), F32)
        gate = jnp.zeros((rows, toks), F32)
        for k in range(ids_ref.shape[0]):
            same = ids_ref[k : k + 1, :] == expert
            hit = jnp.where(same, 1.0, hit)
            gate = jnp.where(same, gates_ref[k : k + 1, :], gate)
        earlier = onehot(
            lax.broadcasted_iota(jnp.int32, (toks, toks), 0) < lax.broadcasted_iota(jnp.int32, (toks, toks), 1)
        )
        slot = dot(hit.astype(BF), earlier)
        want = jnp.bitwise_and(ci, CAP - 1).astype(F32)
        kept = jnp.where(slot == want, hit, 0.0)
        gate = gate * kept
        pick[...] = kept.astype(BF)
        pick_t[...] = kept.T.astype(BF)
        mixed = gate.T
        high = mixed.astype(BF)
        mix_hi[...] = high
        mix_lo[...] = (mixed - high.astype(F32)).astype(BF)
        return jnp.sum(gate, axis=1, keepdims=True)

    def columns(n, base=0):
        return slice(base + tile * n, base + tile * (n + 1))

    def lanes(j):
        return slice(LANE * j, LANE * (j + 1))

    def make_rows():
        load_tok.wait()
        for n in range(dp // tile):
            rows_nat[:, columns(n)] = dot(pick[...], tok[columns(n), :], NT).astype(BF)
        for j in range(dp // LANE):
            rows_send[:, lanes(j)] = pick_columns(rows_nat, 1, j).astype(BF)

    def make_grads(slot_gate):
        load_cot.wait()
        for n in range(dp // tile):
            grads_send[:, columns(n)] = (dot(pick[...], cot[columns(n), :], NT) * slot_gate).astype(BF)

    def activate(at, act, upper):
        here = slice(at, at + act.shape[1])
        sigma = jax.nn.sigmoid(act)
        gated = act * sigma
        hid[:, here] = (gated * upper).astype(BF)
        slope = upper * sigma * (1.0 + act * (1.0 - sigma))
        for value, high_ref, low_ref in ((slope, fac_gate_hi, fac_gate_lo), (gated, fac_up_hi, fac_up_lo)):
            high = value.astype(BF)
            high_ref[:, here] = high
            low_ref[:, here] = (value - high.astype(F32)).astype(BF)

    def forward_main(n):
        activate(
            tile * n, dot(rows_in[...], weights[:, columns(n)]), dot(rows_in[...], weights[:, columns(n, head)])
        )

    def forward_rest():
        at = 2 * head
        if tail:
            both = dot(rows_in[...], weights[:, at : at + 2 * tail])
            activate(head, both[:, 0:tail], both[:, tail : 2 * tail])
        both = dot(rows_in[...], weights[:, at + 2 * tail : at + 2 * tail + LANE])
        activate(head + tail, both, pltpu.roll(both, LANE - odd, 1))

    def spread(j):
        hid_pad[:, lanes(j)] = pick_columns(hid, 2, j, (head,)).astype(BF)
        fac_gate[:, lanes(j)] = pick_columns(fac_gate_hi, 2, j, (head,)) + pick_columns(fac_gate_lo, 2, j, (head,))
        fac_up[:, lanes(j)] = pick_columns(fac_up_hi, 2, j, (head,)) + pick_columns(fac_up_lo, 2, j, (head,))

    def send_result(n):
        out_send[n] = dot(hid_pad[...], weights[:, first + cw * n : first + cw * (n + 1)]).astype(BF)
        send_back(2 + n, out_send.at[n], out_recv.at[n])

    def backward_part(m, n):
        part = dot(grads_in[:, cw * m : cw * (m + 1)], weights[columns(n), first + cw * m : first + cw * (m + 1)], NT)
        if m > 0:
            part = part + hid_grad[:, columns(n)]
        if m < chunks - 1:
            hid_grad[:, columns(n)] = part
        else:
            pg_gate[:, columns(n)] = (part * fac_gate[:, columns(n)]).astype(BF)
            pg_up[:, columns(n)] = (part * fac_up[:, columns(n)]).astype(BF)

    def pack(j):
        part = None
        for row, src in ((3, pg_gate), (4, pg_up)):
            if (table[row, lanes(j)] >= 0).any():
                more = pick_columns(src, row, j)
                part = more if part is None else part + more
        pg[:, lanes(j)] = part.astype(BF)

    tok[width:dp, :] = jnp.zeros((dp - width, toks), BF)
    cot[0:shift, :] = jnp.zeros((shift, toks), BF)
    cot[shift + width : dp, :] = jnp.zeros((dp - shift - width, toks), BF)
    hid[:, width:dp] = jnp.zeros((rows, dp - width), BF)

    pl.semaphore_wait(barrier, len(near))

    count = len(pieces)
    offsets = cfg["offsets"]
    for p in range(count):
        start_swap(p)
    events = []
    for p in range(count):
        events.append((offsets[p] - 1, 0, p, -1))
        events += [(offsets[p] + k, 1, p, k) for k in range(kb)]
        events.append((offsets[p] + kb, 2, p, kb))
    events.sort()
    work = []

    def run(n):
        for _ in range(min(n, len(work))):
            work.pop(0)()

    held = {}

    def prepare_rows():
        held["gate"] = make_slots()
        make_rows()

    def launch_rows():
        send_out(0, rows_send, rows_in)

    def launch_grads():
        make_grads(held["gate"])
        send_out(1, grads_send, grads_in)

    needed = cfg["needed"]
    tiles = dp // tile
    visits = {(r % needed, r // needed): r for r in range(bits + 1)}
    launch = ((bits + 1) % needed, (bits + 1) // needed)
    ended = set()
    round_signal(0)
    for _, _, p, k in events:
        if k == kb and p >= needed:
            run(len(work))
        if k < 0:
            ring_open(p)
        elif k < kb:
            ring_step(p, k)
        else:
            ring_close(p)
            ended.add(p)
        if (p, k) in visits:
            r = visits[p, k]
            round_wait(r)
            if r < bits:
                round_signal(r + 1)
        if (p, k) == (needed - 1, 0):
            prepare_rows()
        if (p, k) == launch:
            launch_rows()
        if (p, k) == (launch[0], launch[1] + 1):
            launch_grads()
        if k == kb and p == needed - 1:
            for q in range(needed):
                ring_here(q)
            wait_for(rows_in, a2a_recv_sem.at[0])
            work += [functools.partial(forward_main, n) for n in range(head // tile)] + [forward_rest]
            work += [functools.partial(spread, j) for j in range(dp // LANE)]
            work += [functools.partial(send_result, 0)]
            work += [functools.partial(wait_for, grads_in, a2a_recv_sem.at[1])]
            work += [functools.partial(backward_part, 0, n) for n in range(tiles)]
        elif ended >= set(range(needed)) and k < kb and p == count - 1:
            run(4)
        if k == kb and p >= needed:
            n = p - needed + 1
            ring_here(p)
            send_result(n)
            for m in range(tiles):
                backward_part(n, m)
    for j in range(pl.cdiv(2 * width, LANE)):
        pack(j)
    wide = pl.cdiv(2 * width, LANE) * LANE
    for n in range(chunks):
        for m in range(cw // tile):
            here = slice(cw * n + tile * m, cw * n + tile * (m + 1))
            rg_send[n, :, columns(m)] = dot(pg[...], weights[here, 0:wide], NT).astype(BF)
        send_back(2 + chunks + n, rg_send.at[n], rg_recv.at[n])

    eye = onehot(
        lax.broadcasted_iota(jnp.int32, (LANE, LANE), 0) == lax.broadcasted_iota(jnp.int32, (LANE, LANE), 1)
    )
    for n in range(chunks):
        wait_for(out_recv.at[n], a2a_recv_sem.at[2 + n])
        summed = (dot(mix_hi[...], out_recv[n]) + dot(mix_lo[...], out_recv[n])).astype(BF)
        for m in range(cw // LANE):
            d = cw * n + LANE * m - shift
            lo, hi = max(d, 0), min(d + LANE, width)
            if hi > lo:
                turned = dot(eye, summed[:, lanes(m)], NT).astype(BF)
                out_ref[lo:hi, :] = turned[lo - d : hi - d, :]
    for n in range(chunks):
        wait_for(rg_recv.at[n], a2a_recv_sem.at[2 + chunks + n])
        rows_nat[:, cw * n : cw * (n + 1)] = dot(pick_t[...], rg_recv[n]).astype(BF)
    for j in range(pl.cdiv(width, LANE)):
        d = np.arange(LANE * j, min(width, LANE * (j + 1)))
        p = pad * (d // per) + d % per
        start = int(p.min()) // LANE * LANE
        stop = (int(p.max()) // LANE + 1) * LANE
        di = lax.broadcasted_iota(jnp.int32, (LANE, stop - start), 0) + LANE * j
        sel = onehot(di == table_ref[1:2, start:stop])
        turned = dot(sel, rows_nat[:, start:stop], NT).astype(BF)
        igrad_ref[LANE * j : LANE * j + len(d), :] = turned[0 : len(d), :]

    for p in range(count):
        for way in range(2):
            wait_for(piece(p, 0, kb * pad), ring_send_sem.at[p, way])
        wait_for(piece(p, 0, pad), last_send_sem.at[p])
        wait_for(piece(p, 0, nz * pad), sib_send_sem.at[p])

        @pl.when(swaps)
        def _():
            wait_for(own_piece(p), swap_send.at[p])

    sent(0, rows_send)
    sent(1, grads_send)
    for n in range(chunks):
        sent(2 + n, out_send.at[n])
        sent(2 + chunks + n, rg_send.at[n])


def shards(mesh_shape, tokens, cotangent, expert_ids, gates, gate_up_weight, down_matrix):
    ne = mesh_shape["expert"]
    nz = mesh_shape["fsdp"] // 2
    toks, width = tokens.shape
    per = down_matrix.shape[1]
    pad = pl.cdiv(per, 16) * 16
    cfg = tables(nz, per, pad, width)
    dp, total, head, first = cfg["dp"], cfg["total"], cfg["head"], cfg["first"]
    chunks = 3
    cw = dp // chunks
    tile = 256 if cw % 256 == 0 and head % 256 == 0 else 128
    rows = ne * CAP
    pieces = [(0, head), (head, head), (2 * head, first + cw - 2 * head), (first + cw, cw), (first + 2 * cw, cw)]
    cfg.update(nz=nz, ne=ne, per=per, pad=pad, width=width, tile=tile, pieces=pieces, needed=3, offsets=(0, 0, 0, 1, 1))
    any_spec = pl.BlockSpec(memory_space=pl.ANY)
    vmem_spec = pl.BlockSpec(memory_space=pltpu.VMEM)
    dma = pltpu.SemaphoreType.DMA
    flat = (rows, dp)
    wide = pl.cdiv(2 * width, LANE) * LANE
    count = len(pieces)
    out_t, grad_t = pl.pallas_call(
        functools.partial(layer_kernel, cfg),
        out_shape=[jax.ShapeDtypeStruct((width, toks), BF)] * 2,
        in_specs=[any_spec] * 4 + [vmem_spec] * 3,
        out_specs=[vmem_spec] * 2,
        scratch_shapes=[
            pltpu.VMEM((per, 2 * width), BF),
            pltpu.VMEM((per, width), BF),
            pltpu.VMEM((pad, total), F32),
            pltpu.VMEM((pad, total), BF),
            pltpu.VMEM((dp, total), BF),
            pltpu.VMEM((dp, toks), BF),
            pltpu.VMEM((dp, toks), BF),
            pltpu.VMEM((toks, dp), BF),
        ]
        + [pltpu.VMEM(flat, BF)] * 10
        + [pltpu.VMEM(flat, F32)] * 3
        + [pltpu.VMEM(flat, BF)] * 2
        + [pltpu.VMEM((rows, wide), BF)]
        + [pltpu.VMEM((chunks, rows, cw), BF)] * 4
        + [
            pltpu.VMEM((rows, toks), BF),
            pltpu.VMEM((toks, rows), BF),
            pltpu.VMEM((toks, rows), BF),
            pltpu.VMEM((toks, rows), BF),
            dma((4,)),
            dma((count,)),
            dma((count,)),
            dma((count, 2)),
            dma((count, 2, nz // 2)),
            dma((count,)),
            dma((count,)),
            dma((count,)),
            dma((count,)),
            dma((2 + 2 * chunks,)),
            dma((2 + 2 * chunks,)),
            pltpu.SemaphoreType.REGULAR((ne.bit_length(),)),
        ],
        compiler_params=pltpu.CompilerParams(
            collective_id=0, has_side_effects=True, vmem_limit_bytes=60 * 1024 * 1024
        ),
    )(gate_up_weight[0], down_matrix[0], tokens.T, cotangent.T, expert_ids.T, gates.T, jnp.asarray(cfg["table"]))
    return out_t.T, grad_t.T


def solution(mesh):
    in_specs = (
        P(("fsdp", "expert"), None),
        P(("fsdp", "expert"), None),
        P(("fsdp", "expert"), None),
        P(("fsdp", "expert"), None),
        P("expert", "fsdp", None),
        P("expert", "fsdp", None),
    )
    out_specs = (P(("fsdp", "expert"), None), P(("fsdp", "expert"), None))
    return jax.shard_map(
        functools.partial(shards, dict(mesh.shape)), mesh=mesh, in_specs=in_specs, out_specs=out_specs, check_vma=False
    )
```

```python
import functools

import jax
import jax.numpy as jnp
import numpy as np
from jax import lax
from jax.experimental import pallas as pl
from jax.experimental.pallas import tpu as pltpu
from jax.sharding import PartitionSpec as P

MESH = pl.DeviceIdType.MESH
CAP = 16
LANE = 128
BF = jnp.bfloat16
F32 = jnp.float32
NN = (((1,), (0,)), ((), ()))
NT = (((1,), (1,)), ((), ()))


def dot(a, b, dims=NN):
    return lax.dot_general(a, b, dims, preferred_element_type=F32)


def onehot(mask):
    return jnp.where(mask, 1.0, 0.0).astype(BF)


def windows(idx, width, cuts):
    edges = [0, *cuts, width]
    found = []
    for lo, hi in zip(edges[:-1], edges[1:]):
        part = idx[(idx >= lo) & (idx < hi)]
        if part.size:
            start = int(part.min()) // LANE * LANE
            found.append((start, min(pl.cdiv(int(part.max()) + 1, LANE) * LANE, hi)))
    return found


def tables(nz, per, pad, width):
    ns = 2 * nz
    dp = ns * pad
    main = per // 8 * 8
    rest = per - main
    head = ns * main
    q = np.arange(width)
    s = np.where(q < head, q // main, (q - head) // rest)
    i = np.where(q < head, q % main, main + (q - head) % rest)
    nat_q, pad_q = per * s + i, pad * s + i
    p = np.arange(dp)
    place = np.where(p % pad < per, per * (p // pad) + p % pad, -1)
    packed_p = np.full(dp, -1)
    packed_p[pad_q] = q
    tail = (width - head) // LANE * LANE
    odd = width - head - tail
    gate_q = np.concatenate([np.arange(head), 2 * head + np.arange(tail), 2 * head + 2 * tail + np.arange(odd)])
    up_q = np.concatenate([head + np.arange(head), 2 * head + tail + np.arange(tail), 2 * head + 2 * tail + odd + np.arange(odd)])
    down_at = 2 * width
    total = pl.cdiv(3 * width, LANE) * LANE
    first = down_at // LANE * LANE
    assert total - first == dp and head % LANE == 0
    own = np.full(total, -1)
    own[gate_q] = nat_q
    own[up_q] = width + nat_q
    from_gate = np.full(total, -1)
    from_gate[gate_q] = pad_q
    from_up = np.full(total, -1)
    from_up[up_q] = pad_q
    table = np.full((8, total), -1, np.int32)
    table[0], table[1, :dp], table[2, :dp], table[3], table[4] = own, place, packed_p, from_gate, from_up
    return dict(head=head, tail=tail, odd=odd, first=first, shift=down_at - first, total=total, dp=dp, table=table)


def layer_kernel(
    cfg,
    gate_up_hbm, down_hbm, tok_hbm, cot_hbm, ids_ref, gates_ref, table_ref,
    out_ref, igrad_ref,
    gu_own, dn_own, own32, own, weights,
    tok, cot, rows_nat, rows_send, rows_in, grads_send, grads_in,
    hid, fac_gate_hi, fac_gate_lo, fac_up_hi, fac_up_lo, hid_pad, fac_gate, fac_up, hid_grad, pg_gate, pg_up, pg,
    out_send, rg_send, out_recv, rg_recv,
    pick, pick_t, mix_hi, mix_lo,
    in_sem, swap_send, swap_recv, ring_send_sem, ring_recv_sem, last_send_sem, last_recv_sem,
    sib_send_sem, sib_recv_sem, a2a_send_sem, a2a_recv_sem, round_sem,
):
    nz, ne, per, pad, width = cfg["nz"], cfg["ne"], cfg["per"], cfg["pad"], cfg["width"]
    head, tail, odd, first, shift = cfg["head"], cfg["tail"], cfg["odd"], cfg["first"], cfg["shift"]
    dp, total, table, pieces = cfg["dp"], cfg["total"], cfg["table"], cfg["pieces"]
    chunks, rows, cw = out_send.shape
    tile = cfg["tile"]
    toks = ids_ref.shape[1]
    kb = nz // 2 - 1

    f = lax.axis_index("fsdp")
    e = lax.axis_index("expert")
    ylo = lax.div(f, nz)
    z = lax.rem(f, nz)
    c = lax.rem(e, 2)
    e2 = lax.div(e, 2)
    keeps = ylo == c
    swaps = ylo != c
    znext = ylo * nz + lax.rem(z + 1, nz)
    zprev = ylo * nz + lax.rem(z + nz - 1, nz)

    bits = ne.bit_length() - 1
    partners = [((1 - ylo) * nz + z, e)]
    for r in range(bits):
        bit = lax.rem(lax.div(e, 2**r), 2)
        partners.append((f, e + (1 - 2 * bit) * 2**r))
    swap_partner = ((1 - ylo) * nz + z, e2 * 2 + 1 - c)
    barrier = pltpu.get_barrier_semaphore()
    near = [(znext, e), (zprev, e), swap_partner] + partners
    for there in near:
        pl.semaphore_signal(barrier, inc=1, device_id=there, device_id_type=MESH)

    def round_signal(r):
        pl.semaphore_signal(round_sem.at[r], inc=1, device_id=partners[r], device_id_type=MESH)

    def round_wait(r):
        pl.semaphore_wait(round_sem.at[r], 1)

    load_gu = pltpu.make_async_copy(gate_up_hbm, gu_own, in_sem.at[0])
    load_dn = pltpu.make_async_copy(down_hbm, dn_own, in_sem.at[1])
    load_tok = pltpu.make_async_copy(tok_hbm, tok.at[pl.ds(0, width)], in_sem.at[2])
    load_cot = pltpu.make_async_copy(cot_hbm, cot.at[pl.ds(shift, width)], in_sem.at[3])
    load_gu.start()
    load_dn.start()
    load_tok.start()
    load_cot.start()

    def pick_columns(src, row, j, cuts=(), size=LANE):
        acc = None
        for start, stop in windows(table[row, size * j : size * (j + 1)], src.shape[1], cuts):
            col = lax.broadcasted_iota(jnp.int32, (stop - start, size), 0) + start
            part = dot(src[:, start:stop], onehot(col == table_ref[row : row + 1, size * j : size * (j + 1)]))
            acc = part if acc is None else acc + part
        return acc

    own32[...] = jnp.zeros_like(own32)
    load_gu.wait()
    load_dn.wait()
    for j in range(total // LANE):
        part = None
        if (table[0, LANE * j : LANE * (j + 1)] >= 0).any():
            part = pick_columns(gu_own, 0, j, (width // LANE * LANE,))
        lo = max(LANE * j - 2 * width, 0)
        hi = min(LANE * (j + 1) - 2 * width, width)
        if hi > 0:
            start, stop = lo // LANE * LANE, min(pl.cdiv(hi, LANE) * LANE, width)
            col = lax.broadcasted_iota(jnp.int32, (stop - start, LANE), 0) + (start + 2 * width)
            lane = lax.broadcasted_iota(jnp.int32, (stop - start, LANE), 1) + LANE * j
            more = dot(dn_own[:, start:stop], onehot(col == lane))
            part = more if part is None else part + more
        own32[0:per, LANE * j : LANE * (j + 1)] = part
    own[...] = own32[...].astype(BF)

    def piece(p, at, size):
        start, wide = pieces[p]
        return weights.at[pl.ds(pl.multiple_of(at, 16), size), pl.ds(start, wide)]

    def own_piece(p):
        start, wide = pieces[p]
        return own.at[:, pl.ds(start, wide)]

    def block(p, core, b):
        return piece(p, (core * nz + b) * pad, pad)

    def wait_for(ref, sem):
        pltpu.make_async_copy(ref, ref, sem).wait()

    def start_swap(p):
        @pl.when(keeps)
        def _():
            pltpu.make_async_copy(own_piece(p), block(p, c, z), swap_recv.at[p]).start()

        @pl.when(swaps)
        def _():
            pltpu.make_async_remote_copy(
                src_ref=own_piece(p), dst_ref=block(p, 1 - c, z),
                send_sem=swap_send.at[p], recv_sem=swap_recv.at[p],
                device_id=swap_partner, device_id_type=MESH,
            ).start()

    def ring_send(p, way, k):
        b = lax.rem(z + nz - k, nz) if way == 0 else lax.rem(z + k, nz)
        pltpu.make_async_remote_copy(
            src_ref=block(p, c, b), dst_ref=block(p, c, b),
            send_sem=ring_send_sem.at[p, way], recv_sem=ring_recv_sem.at[p, way, k],
            device_id=(znext if way == 0 else zprev, e), device_id_type=MESH,
        ).start()

    def last_send(p):
        b = lax.rem(z + nz - (1 - 2 * c) * kb, nz)
        pltpu.make_async_remote_copy(
            src_ref=block(p, c, b), dst_ref=block(p, c, b),
            send_sem=last_send_sem.at[p], recv_sem=last_recv_sem.at[p],
            device_id=(ylo * nz + lax.rem(z + nz + 1 - 2 * c, nz), e), device_id_type=MESH,
        ).start()

    def sib_send(p, b):
        pltpu.make_async_remote_copy(
            src_ref=block(p, c, b), dst_ref=block(p, c, b),
            send_sem=sib_send_sem.at[p], recv_sem=sib_recv_sem.at[p],
            device_id=(f, e2 * 2 + 1 - c), device_id_type=MESH,
        ).start()

    def ring_open(p):
        wait_for(block(p, c, z), swap_recv.at[p])
        ring_send(p, 0, 0)
        ring_send(p, 1, 0)
        sib_send(p, z)

    def ring_step(p, k):
        came = (lax.rem(z + nz - 1 - k, nz), lax.rem(z + 1 + k, nz))
        for way in range(2):
            wait_for(block(p, c, came[way]), ring_recv_sem.at[p, way, k])
            if k < kb - 1:
                ring_send(p, way, k + 1)
            sib_send(p, came[way])
        if k == kb - 1:
            last_send(p)

    def ring_close(p):
        b = lax.rem(z + nz // 2, nz)
        wait_for(block(p, c, b), last_recv_sem.at[p])
        sib_send(p, b)

    def ring_here(p):
        wait_for(piece(p, (1 - c) * nz * pad, nz * pad), sib_recv_sem.at[p])

    def go(i, src, dst, gf, ge):
        @pl.when((gf != f) | (ge != e))
        def _():
            pltpu.make_async_remote_copy(
                src_ref=src, dst_ref=dst, send_sem=a2a_send_sem.at[i], recv_sem=a2a_recv_sem.at[i],
                device_id=(gf, ge), device_id_type=MESH,
            ).start()

        @pl.when((gf == f) & (ge == e))
        def _():
            pltpu.make_async_copy(src, dst, a2a_recv_sem.at[i]).start()

    def sixteen(ref, i):
        return ref.at[pl.ds(pl.multiple_of(i * CAP, CAP), CAP)]

    def send_out(i, src, dst):
        def one(t, _):
            x = lax.rem(e + t, ne)
            go(i, sixteen(src, x), sixteen(dst, e), lax.rem(x, 2) * nz + z, lax.div(x, 2) * 2 + ylo)
            return 0

        lax.fori_loop(0, ne, one, 0)

    def send_back(i, src, dst):
        def one(t, _):
            x = lax.rem(e + ne // 2 + lax.div(t, 2) * (1 - 2 * lax.rem(t, 2)) - lax.rem(t, 2) + ne, ne)
            go(i, sixteen(src, x), sixteen(dst, e2 * 2 + ylo), c * nz + z, x)
            return 0

        lax.fori_loop(0, ne, one, 0)

    def sent(i, src):
        @pl.when(keeps)
        def _():
            wait_for(src.at[pl.ds(0, rows - CAP)], a2a_send_sem.at[i])

        @pl.when(swaps)
        def _():
            wait_for(src, a2a_send_sem.at[i])

    def make_slots():
        ci = lax.broadcasted_iota(jnp.int32, (rows, toks), 0)
        expert = lax.shift_right_logical(ci, 4)
        hit = jnp.zeros((rows, toks), F32)
        gate = jnp.zeros((rows, toks), F32)
        for k in range(ids_ref.shape[0]):
            same = ids_ref[k : k + 1, :] == expert
            hit = jnp.where(same, 1.0, hit)
            gate = jnp.where(same, gates_ref[k : k + 1, :], gate)
        earlier = onehot(
            lax.broadcasted_iota(jnp.int32, (toks, toks), 0) < lax.broadcasted_iota(jnp.int32, (toks, toks), 1)
        )
        slot = dot(hit.astype(BF), earlier)
        want = jnp.bitwise_and(ci, CAP - 1).astype(F32)
        kept = jnp.where(slot == want, hit, 0.0)
        gate = gate * kept
        pick[...] = kept.astype(BF)
        pick_t[...] = kept.T.astype(BF)
        mixed = gate.T
        high = mixed.astype(BF)
        mix_hi[...] = high
        mix_lo[...] = (mixed - high.astype(F32)).astype(BF)
        return jnp.sum(gate, axis=1, keepdims=True)

    def columns(n, base=0):
        return slice(base + tile * n, base + tile * (n + 1))

    def lanes(j):
        return slice(LANE * j, LANE * (j + 1))

    def make_rows():
        load_tok.wait()
        for n in range(dp // tile):
            rows_nat[:, columns(n)] = dot(pick[...], tok[columns(n), :], NT).astype(BF)
        for j in range(dp // LANE):
            rows_send[:, lanes(j)] = pick_columns(rows_nat, 1, j).astype(BF)

    def make_grads(slot_gate):
        load_cot.wait()
        for n in range(dp // tile):
            grads_send[:, columns(n)] = (dot(pick[...], cot[columns(n), :], NT) * slot_gate).astype(BF)

    def activate(at, act, upper):
        here = slice(at, at + act.shape[1])
        sigma = jax.nn.sigmoid(act)
        gated = act * sigma
        hid[:, here] = (gated * upper).astype(BF)
        slope = upper * sigma * (1.0 + act * (1.0 - sigma))
        for value, high_ref, low_ref in ((slope, fac_gate_hi, fac_gate_lo), (gated, fac_up_hi, fac_up_lo)):
            high = value.astype(BF)
            high_ref[:, here] = high
            low_ref[:, here] = (value - high.astype(F32)).astype(BF)

    def forward_main(n):
        activate(
            tile * n, dot(rows_in[...], weights[:, columns(n)]), dot(rows_in[...], weights[:, columns(n, head)])
        )

    def forward_rest():
        at = 2 * head
        if tail:
            both = dot(rows_in[...], weights[:, at : at + 2 * tail])
            activate(head, both[:, 0:tail], both[:, tail : 2 * tail])
        both = dot(rows_in[...], weights[:, at + 2 * tail : at + 2 * tail + LANE])
        activate(head + tail, both, pltpu.roll(both, LANE - odd, 1))

    def spread(j):
        here = columns(j)
        hid_pad[:, here] = pick_columns(hid, 2, j, (head,), tile).astype(BF)
        fac_gate[:, here] = pick_columns(fac_gate_hi, 2, j, (head,), tile) + pick_columns(fac_gate_lo, 2, j, (head,), tile)
        fac_up[:, here] = pick_columns(fac_up_hi, 2, j, (head,), tile) + pick_columns(fac_up_lo, 2, j, (head,), tile)

    def send_result(n):
        out_send[n] = dot(hid_pad[...], weights[:, first + cw * n : first + cw * (n + 1)]).astype(BF)
        send_back(2 + n, out_send.at[n], out_recv.at[n])

    def backward_part(m, n):
        part = dot(grads_in[:, cw * m : cw * (m + 1)], weights[columns(n), first + cw * m : first + cw * (m + 1)], NT)
        if m > 0:
            part = part + hid_grad[:, columns(n)]
        if m < chunks - 1:
            hid_grad[:, columns(n)] = part
        else:
            pg_gate[:, columns(n)] = (part * fac_gate[:, columns(n)]).astype(BF)
            pg_up[:, columns(n)] = (part * fac_up[:, columns(n)]).astype(BF)

    def pack(j, size):
        part = None
        here = slice(size * j, size * (j + 1))
        for row, src in ((3, pg_gate), (4, pg_up)):
            if (table[row, here] >= 0).any():
                more = pick_columns(src, row, j, (), size)
                part = more if part is None else part + more
        pg[:, here] = part.astype(BF)

    tok[width:dp, :] = jnp.zeros((dp - width, toks), BF)
    cot[0:shift, :] = jnp.zeros((shift, toks), BF)
    cot[shift + width : dp, :] = jnp.zeros((dp - shift - width, toks), BF)
    hid[:, width:dp] = jnp.zeros((rows, dp - width), BF)

    pl.semaphore_wait(barrier, len(near))

    count = len(pieces)
    offsets = cfg["offsets"]
    for p in range(count):
        start_swap(p)
    events = []
    for p in range(count):
        events.append((offsets[p] - 1, 0, p, -1))
        events += [(offsets[p] + k, 1, p, k) for k in range(kb)]
        events.append((offsets[p] + kb, 2, p, kb))
    events.sort()
    work = []

    def run(n):
        for _ in range(min(n, len(work))):
            work.pop(0)()

    held = {}

    def prepare_rows():
        held["gate"] = make_slots()
        make_rows()

    def launch_rows():
        send_out(0, rows_send, rows_in)

    def launch_grads():
        make_grads(held["gate"])
        send_out(1, grads_send, grads_in)

    needed = cfg["needed"]
    tiles = dp // tile
    steps = 0
    ended = set()
    round_signal(0)
    for _, _, p, k in events:
        if k == kb and p >= needed:
            run(len(work))
        if k < 0:
            ring_open(p)
        elif k < kb:
            ring_step(p, k)
        else:
            ring_close(p)
            ended.add(p)
        if 0 <= k < kb:
            if steps <= bits:
                round_wait(steps)
                if steps < bits:
                    round_signal(steps + 1)
            if steps == 2:
                prepare_rows()
            if steps == bits + 1:
                launch_rows()
            if steps == bits + 3:
                launch_grads()
            steps += 1
        if k == kb and p == needed - 2:
            for q in range(needed - 1):
                ring_here(q)
            wait_for(rows_in, a2a_recv_sem.at[0])
            work += [functools.partial(forward_main, n) for n in range(head // tile)]
        elif k == kb and p == needed - 1:
            run(len(work))
            ring_here(p)
            work += [forward_rest] + [functools.partial(spread, j) for j in range(tiles)]
            work += [functools.partial(send_result, 0)]
            work += [functools.partial(wait_for, grads_in, a2a_recv_sem.at[1])]
            work += [functools.partial(backward_part, 0, n) for n in range(tiles)]
        elif p >= min(needed - 1, count - 1) and k < kb:
            run(cfg["burst"])
        if k == kb and p >= needed:
            n = p - needed + 1
            ring_here(p)
            send_result(n)
            for m in range(tiles):
                backward_part(n, m)
    for j in range(2 * head // tile):
        pack(j, tile)
    for j in range(2 * head // LANE, pl.cdiv(2 * width, LANE)):
        pack(j, LANE)
    wide = pl.cdiv(2 * width, LANE) * LANE
    for n in range(chunks):
        for m in range(cw // tile):
            here = slice(cw * n + tile * m, cw * n + tile * (m + 1))
            rg_send[n, :, columns(m)] = dot(pg[...], weights[here, 0:wide], NT).astype(BF)
        send_back(2 + chunks + n, rg_send.at[n], rg_recv.at[n])

    eye = onehot(
        lax.broadcasted_iota(jnp.int32, (LANE, LANE), 0) == lax.broadcasted_iota(jnp.int32, (LANE, LANE), 1)
    )
    for n in range(chunks):
        wait_for(out_recv.at[n], a2a_recv_sem.at[2 + n])
        summed = (dot(mix_hi[...], out_recv[n]) + dot(mix_lo[...], out_recv[n])).astype(BF)
        for m in range(cw // LANE):
            d = cw * n + LANE * m - shift
            lo, hi = max(d, 0), min(d + LANE, width)
            if hi > lo:
                turned = dot(eye, summed[:, lanes(m)], NT).astype(BF)
                out_ref[lo:hi, :] = turned[lo - d : hi - d, :]
    for n in range(chunks):
        wait_for(rg_recv.at[n], a2a_recv_sem.at[2 + chunks + n])
        rows_nat[:, cw * n : cw * (n + 1)] = dot(pick_t[...], rg_recv[n]).astype(BF)
    for j in range(pl.cdiv(width, LANE)):
        d = np.arange(LANE * j, min(width, LANE * (j + 1)))
        p = pad * (d // per) + d % per
        start = int(p.min()) // LANE * LANE
        stop = (int(p.max()) // LANE + 1) * LANE
        di = lax.broadcasted_iota(jnp.int32, (LANE, stop - start), 0) + LANE * j
        sel = onehot(di == table_ref[1:2, start:stop])
        turned = dot(sel, rows_nat[:, start:stop], NT).astype(BF)
        igrad_ref[LANE * j : LANE * j + len(d), :] = turned[0 : len(d), :]

    for p in range(count):
        for way in range(2):
            wait_for(piece(p, 0, kb * pad), ring_send_sem.at[p, way])
        wait_for(piece(p, 0, pad), last_send_sem.at[p])
        wait_for(piece(p, 0, nz * pad), sib_send_sem.at[p])

        @pl.when(swaps)
        def _():
            wait_for(own_piece(p), swap_send.at[p])

    sent(0, rows_send)
    sent(1, grads_send)
    for n in range(chunks):
        sent(2 + n, out_send.at[n])
        sent(2 + chunks + n, rg_send.at[n])


def shards(mesh_shape, tokens, cotangent, expert_ids, gates, gate_up_weight, down_matrix):
    ne = mesh_shape["expert"]
    nz = mesh_shape["fsdp"] // 2
    toks, width = tokens.shape
    per = down_matrix.shape[1]
    pad = pl.cdiv(per, 16) * 16
    cfg = tables(nz, per, pad, width)
    dp, total, head, first = cfg["dp"], cfg["total"], cfg["head"], cfg["first"]
    chunks = 3
    cw = dp // chunks
    tile = 256 if cw % 256 == 0 and head % 256 == 0 else 128
    rows = ne * CAP
    pieces = [(0, head), (head, head), (2 * head, first + cw - 2 * head), (first + cw, cw), (first + 2 * cw, cw)]
    cfg.update(nz=nz, ne=ne, per=per, pad=pad, width=width, tile=tile, pieces=pieces, needed=3, offsets=(0, 0, 1, 3, 3), burst=1)
    any_spec = pl.BlockSpec(memory_space=pl.ANY)
    vmem_spec = pl.BlockSpec(memory_space=pltpu.VMEM)
    dma = pltpu.SemaphoreType.DMA
    flat = (rows, dp)
    wide = pl.cdiv(2 * width, LANE) * LANE
    count = len(pieces)
    out_t, grad_t = pl.pallas_call(
        functools.partial(layer_kernel, cfg),
        out_shape=[pltpu.VMEM((width, toks), BF)] * 2,
        in_specs=[any_spec] * 4 + [vmem_spec] * 3,
        out_specs=[vmem_spec] * 2,
        scratch_shapes=[
            pltpu.VMEM((per, 2 * width), BF),
            pltpu.VMEM((per, width), BF),
            pltpu.VMEM((pad, total), F32),
            pltpu.VMEM((pad, total), BF),
            pltpu.VMEM((dp, total), BF),
            pltpu.VMEM((dp, toks), BF),
            pltpu.VMEM((dp, toks), BF),
            pltpu.VMEM((toks, dp), BF),
        ]
        + [pltpu.VMEM(flat, BF)] * 10
        + [pltpu.VMEM(flat, F32)] * 3
        + [pltpu.VMEM(flat, BF)] * 2
        + [pltpu.VMEM((rows, wide), BF)]
        + [pltpu.VMEM((chunks, rows, cw), BF)] * 4
        + [
            pltpu.VMEM((rows, toks), BF),
            pltpu.VMEM((toks, rows), BF),
            pltpu.VMEM((toks, rows), BF),
            pltpu.VMEM((toks, rows), BF),
            dma((4,)),
            dma((count,)),
            dma((count,)),
            dma((count, 2)),
            dma((count, 2, nz // 2)),
            dma((count,)),
            dma((count,)),
            dma((count,)),
            dma((count,)),
            dma((2 + 2 * chunks,)),
            dma((2 + 2 * chunks,)),
            pltpu.SemaphoreType.REGULAR((ne.bit_length(),)),
        ],
        compiler_params=pltpu.CompilerParams(
            collective_id=0, has_side_effects=True, vmem_limit_bytes=60 * 1024 * 1024
        ),
    )(gate_up_weight[0], down_matrix[0], tokens.T, cotangent.T, expert_ids.T, gates.T, jnp.asarray(cfg["table"]))
    return out_t.T, grad_t.T


def solution(mesh):
    in_specs = (
        P(("fsdp", "expert"), None),
        P(("fsdp", "expert"), None),
        P(("fsdp", "expert"), None),
        P(("fsdp", "expert"), None),
        P("expert", "fsdp", None),
        P("expert", "fsdp", None),
    )
    out_specs = (P(("fsdp", "expert"), None), P(("fsdp", "expert"), None))
    return jax.shard_map(
        functools.partial(shards, dict(mesh.shape)), mesh=mesh, in_specs=in_specs, out_specs=out_specs, check_vma=False
    )
```

```python
import functools

import jax
import jax.numpy as jnp
import numpy as np
from jax import lax
from jax.experimental import pallas as pl
from jax.experimental.pallas import tpu as pltpu
from jax.sharding import PartitionSpec as P

MESH = pl.DeviceIdType.MESH
CAP = 16
LANE = 128
BF = jnp.bfloat16
F32 = jnp.float32
NN = (((1,), (0,)), ((), ()))
NT = (((1,), (1,)), ((), ()))


def dot(a, b, dims=NN):
    return lax.dot_general(a, b, dims, preferred_element_type=F32)


def onehot(mask):
    return jnp.where(mask, 1.0, 0.0).astype(BF)


def windows(idx, width, cuts):
    edges = [0, *cuts, width]
    found = []
    for lo, hi in zip(edges[:-1], edges[1:]):
        part = idx[(idx >= lo) & (idx < hi)]
        if part.size:
            start = int(part.min()) // LANE * LANE
            found.append((start, min(pl.cdiv(int(part.max()) + 1, LANE) * LANE, hi)))
    return found


def tables(nz, per, pad, width):
    ns = 2 * nz
    dp = ns * pad
    main = per // 8 * 8
    rest = per - main
    head = ns * main
    q = np.arange(width)
    s = np.where(q < head, q // main, (q - head) // rest)
    i = np.where(q < head, q % main, main + (q - head) % rest)
    nat_q, pad_q = per * s + i, pad * s + i
    p = np.arange(dp)
    place = np.where(p % pad < per, per * (p // pad) + p % pad, -1)
    packed_p = np.full(dp, -1)
    packed_p[pad_q] = q
    tail = (width - head) // LANE * LANE
    odd = width - head - tail
    gate_q = np.concatenate([np.arange(head), 2 * head + np.arange(tail), 2 * head + 2 * tail + np.arange(odd)])
    up_q = np.concatenate([head + np.arange(head), 2 * head + tail + np.arange(tail), 2 * head + 2 * tail + odd + np.arange(odd)])
    down_at = 2 * width
    total = pl.cdiv(3 * width, LANE) * LANE
    first = down_at // LANE * LANE
    assert total - first == dp and head % LANE == 0
    own = np.full(total, -1)
    own[gate_q] = nat_q
    own[up_q] = width + nat_q
    from_gate = np.full(total, -1)
    from_gate[gate_q] = pad_q
    from_up = np.full(total, -1)
    from_up[up_q] = pad_q
    table = np.full((8, total), -1, np.int32)
    table[0], table[1, :dp], table[2, :dp], table[3], table[4] = own, place, packed_p, from_gate, from_up
    return dict(head=head, tail=tail, odd=odd, first=first, shift=down_at - first, total=total, dp=dp, table=table)


def layer_kernel(
    cfg,
    gate_up_hbm, down_hbm, tok_hbm, cot_hbm, ids_ref, gates_ref, table_ref,
    out_ref, igrad_ref,
    gu_own, dn_own, own32, own, weights,
    tok, cot, rows_nat, rows_send, rows_in, grads_send, grads_in,
    hid, fac_gate_hi, fac_gate_lo, fac_up_hi, fac_up_lo, hid_pad, fac_gate, fac_up, hid_grad, pg_gate, pg_up, pg,
    out_send, rg_send, out_recv, rg_recv,
    pick, pick_t, mix_hi, mix_lo,
    in_sem, swap_send, swap_recv, ring_send_sem, ring_recv_sem, last_send_sem, last_recv_sem,
    sib_send_sem, sib_recv_sem, a2a_send_sem, a2a_recv_sem, round_sem,
):
    nz, ne, per, pad, width = cfg["nz"], cfg["ne"], cfg["per"], cfg["pad"], cfg["width"]
    head, tail, odd, first, shift = cfg["head"], cfg["tail"], cfg["odd"], cfg["first"], cfg["shift"]
    dp, total, table, pieces = cfg["dp"], cfg["total"], cfg["table"], cfg["pieces"]
    chunks, rows, cw = out_send.shape
    tile = cfg["tile"]
    toks = ids_ref.shape[1]
    kb = nz // 2 - 1

    f = lax.axis_index("fsdp")
    e = lax.axis_index("expert")
    ylo = lax.div(f, nz)
    z = lax.rem(f, nz)
    c = lax.rem(e, 2)
    e2 = lax.div(e, 2)
    keeps = ylo == c
    swaps = ylo != c
    znext = ylo * nz + lax.rem(z + 1, nz)
    zprev = ylo * nz + lax.rem(z + nz - 1, nz)

    bits = ne.bit_length() - 1
    partners = [((1 - ylo) * nz + z, e)]
    for r in range(bits):
        bit = lax.rem(lax.div(e, 2**r), 2)
        partners.append((f, e + (1 - 2 * bit) * 2**r))
    swap_partner = ((1 - ylo) * nz + z, e2 * 2 + 1 - c)
    barrier = pltpu.get_barrier_semaphore()
    near = [(znext, e), (zprev, e), swap_partner] + partners
    for there in near:
        pl.semaphore_signal(barrier, inc=1, device_id=there, device_id_type=MESH)

    def round_signal(r):
        pl.semaphore_signal(round_sem.at[r], inc=1, device_id=partners[r], device_id_type=MESH)

    def round_wait(r):
        pl.semaphore_wait(round_sem.at[r], 1)

    load_gu = pltpu.make_async_copy(gate_up_hbm, gu_own, in_sem.at[0])
    load_dn = pltpu.make_async_copy(down_hbm, dn_own, in_sem.at[1])
    load_tok = pltpu.make_async_copy(tok_hbm, tok.at[pl.ds(0, width)], in_sem.at[2])
    load_cot = pltpu.make_async_copy(cot_hbm, cot.at[pl.ds(shift, width)], in_sem.at[3])
    load_gu.start()
    load_dn.start()
    load_tok.start()
    load_cot.start()

    def pick_columns(src, row, j, cuts=(), size=LANE):
        acc = None
        for start, stop in windows(table[row, size * j : size * (j + 1)], src.shape[1], cuts):
            col = lax.broadcasted_iota(jnp.int32, (stop - start, size), 0) + start
            part = dot(src[:, start:stop], onehot(col == table_ref[row : row + 1, size * j : size * (j + 1)]))
            acc = part if acc is None else acc + part
        return acc

    own32[...] = jnp.zeros_like(own32)
    load_gu.wait()
    load_dn.wait()
    for j in range(total // LANE):
        part = None
        if (table[0, LANE * j : LANE * (j + 1)] >= 0).any():
            part = pick_columns(gu_own, 0, j, (width // LANE * LANE,))
        lo = max(LANE * j - 2 * width, 0)
        hi = min(LANE * (j + 1) - 2 * width, width)
        if hi > 0:
            start, stop = lo // LANE * LANE, min(pl.cdiv(hi, LANE) * LANE, width)
            col = lax.broadcasted_iota(jnp.int32, (stop - start, LANE), 0) + (start + 2 * width)
            lane = lax.broadcasted_iota(jnp.int32, (stop - start, LANE), 1) + LANE * j
            more = dot(dn_own[:, start:stop], onehot(col == lane))
            part = more if part is None else part + more
        own32[0:per, LANE * j : LANE * (j + 1)] = part
    own[...] = own32[...].astype(BF)

    def piece(p, at, size):
        start, wide = pieces[p]
        return weights.at[pl.ds(pl.multiple_of(at, 16), size), pl.ds(start, wide)]

    def own_piece(p):
        start, wide = pieces[p]
        return own.at[:, pl.ds(start, wide)]

    def block(p, core, b):
        return piece(p, (core * nz + b) * pad, pad)

    def wait_for(ref, sem):
        pltpu.make_async_copy(ref, ref, sem).wait()

    def start_swap(p):
        @pl.when(keeps)
        def _():
            pltpu.make_async_copy(own_piece(p), block(p, c, z), swap_recv.at[p]).start()

        @pl.when(swaps)
        def _():
            pltpu.make_async_remote_copy(
                src_ref=own_piece(p), dst_ref=block(p, 1 - c, z),
                send_sem=swap_send.at[p], recv_sem=swap_recv.at[p],
                device_id=swap_partner, device_id_type=MESH,
            ).start()

    def ring_send(p, way, k):
        b = lax.rem(z + nz - k, nz) if way == 0 else lax.rem(z + k, nz)
        pltpu.make_async_remote_copy(
            src_ref=block(p, c, b), dst_ref=block(p, c, b),
            send_sem=ring_send_sem.at[p, way], recv_sem=ring_recv_sem.at[p, way, k],
            device_id=(znext if way == 0 else zprev, e), device_id_type=MESH,
        ).start()

    def last_send(p):
        b = lax.rem(z + nz - (1 - 2 * c) * kb, nz)
        pltpu.make_async_remote_copy(
            src_ref=block(p, c, b), dst_ref=block(p, c, b),
            send_sem=last_send_sem.at[p], recv_sem=last_recv_sem.at[p],
            device_id=(ylo * nz + lax.rem(z + nz + 1 - 2 * c, nz), e), device_id_type=MESH,
        ).start()

    def sib_send(p, b):
        pltpu.make_async_remote_copy(
            src_ref=block(p, c, b), dst_ref=block(p, c, b),
            send_sem=sib_send_sem.at[p], recv_sem=sib_recv_sem.at[p],
            device_id=(f, e2 * 2 + 1 - c), device_id_type=MESH,
        ).start()

    def ring_open(p):
        wait_for(block(p, c, z), swap_recv.at[p])
        ring_send(p, 0, 0)
        ring_send(p, 1, 0)
        sib_send(p, z)

    def ring_step(p, k):
        came = (lax.rem(z + nz - 1 - k, nz), lax.rem(z + 1 + k, nz))
        for way in range(2):
            wait_for(block(p, c, came[way]), ring_recv_sem.at[p, way, k])
            if k < kb - 1:
                ring_send(p, way, k + 1)
            sib_send(p, came[way])
        if k == kb - 1:
            last_send(p)

    def ring_close(p):
        b = lax.rem(z + nz // 2, nz)
        wait_for(block(p, c, b), last_recv_sem.at[p])
        sib_send(p, b)

    def ring_here(p):
        wait_for(piece(p, (1 - c) * nz * pad, nz * pad), sib_recv_sem.at[p])

    def far(i, src, dst, gf, ge):
        pltpu.make_async_remote_copy(
            src_ref=src, dst_ref=dst, send_sem=a2a_send_sem.at[i], recv_sem=a2a_recv_sem.at[i],
            device_id=(gf, ge), device_id_type=MESH,
        ).start()

    def same_place(i, src, dst, gf, ge):
        @pl.when(swaps)
        def _():
            far(i, src, dst, gf, ge)

        @pl.when(keeps)
        def _():
            pltpu.make_async_copy(src, dst, a2a_recv_sem.at[i]).start()

    def others(send):
        def one(t, _):
            x = e + jnp.where(t < ne // 2, t + ne // 2, ne - 1 - t)
            send(jnp.where(x >= ne, x - ne, x))
            return 0

        lax.fori_loop(0, ne - 1, one, 0)

    def sixteen(ref, i):
        return ref.at[pl.ds(pl.multiple_of(i * CAP, CAP), CAP)]

    def send_out(i, src, dst):
        def send(x, put=far):
            odd_x = lax.rem(x, 2)
            put(i, sixteen(src, x), sixteen(dst, e), odd_x * nz + z, x - odd_x + ylo)

        others(send)
        send(e, same_place)

    def send_back(i, src, dst):
        def send(x, put=far):
            put(i, sixteen(src, x), sixteen(dst, e2 * 2 + ylo), c * nz + z, x)

        others(send)
        send(e, same_place)

    def sent(i, src):
        @pl.when(keeps)
        def _():
            wait_for(src.at[pl.ds(0, rows - CAP)], a2a_send_sem.at[i])

        @pl.when(swaps)
        def _():
            wait_for(src, a2a_send_sem.at[i])

    def make_slots():
        ci = lax.broadcasted_iota(jnp.int32, (rows, toks), 0)
        expert = lax.shift_right_logical(ci, 4)
        hit = jnp.zeros((rows, toks), F32)
        gate = jnp.zeros((rows, toks), F32)
        for k in range(ids_ref.shape[0]):
            same = ids_ref[k : k + 1, :] == expert
            hit = jnp.where(same, 1.0, hit)
            gate = jnp.where(same, gates_ref[k : k + 1, :], gate)
        earlier = onehot(
            lax.broadcasted_iota(jnp.int32, (toks, toks), 0) < lax.broadcasted_iota(jnp.int32, (toks, toks), 1)
        )
        slot = dot(hit.astype(BF), earlier)
        want = jnp.bitwise_and(ci, CAP - 1).astype(F32)
        kept = jnp.where(slot == want, hit, 0.0)
        gate = gate * kept
        pick[...] = kept.astype(BF)
        pick_t[...] = kept.T.astype(BF)
        mixed = gate.T
        high = mixed.astype(BF)
        mix_hi[...] = high
        mix_lo[...] = (mixed - high.astype(F32)).astype(BF)
        return jnp.sum(gate, axis=1, keepdims=True)

    def columns(n, base=0):
        return slice(base + tile * n, base + tile * (n + 1))

    def lanes(j):
        return slice(LANE * j, LANE * (j + 1))

    def make_rows():
        load_tok.wait()
        for n in range(dp // tile):
            rows_nat[:, columns(n)] = dot(pick[...], tok[columns(n), :], NT).astype(BF)
        for j in range(dp // LANE):
            rows_send[:, lanes(j)] = pick_columns(rows_nat, 1, j).astype(BF)

    def make_grads(slot_gate):
        load_cot.wait()
        for n in range(dp // tile):
            grads_send[:, columns(n)] = (dot(pick[...], cot[columns(n), :], NT) * slot_gate).astype(BF)

    def activate(at, act, upper):
        here = slice(at, at + act.shape[1])
        sigma = jax.nn.sigmoid(act)
        gated = act * sigma
        hid[:, here] = (gated * upper).astype(BF)
        slope = upper * sigma * (1.0 + act * (1.0 - sigma))
        for value, high_ref, low_ref in ((slope, fac_gate_hi, fac_gate_lo), (gated, fac_up_hi, fac_up_lo)):
            high = value.astype(BF)
            high_ref[:, here] = high
            low_ref[:, here] = (value - high.astype(F32)).astype(BF)

    def forward_main(n):
        activate(
            tile * n, dot(rows_in[...], weights[:, columns(n)]), dot(rows_in[...], weights[:, columns(n, head)])
        )

    def forward_rest():
        at = 2 * head
        if tail:
            both = dot(rows_in[...], weights[:, at : at + 2 * tail])
            activate(head, both[:, 0:tail], both[:, tail : 2 * tail])
        both = dot(rows_in[...], weights[:, at + 2 * tail : at + 2 * tail + LANE])
        activate(head + tail, both, pltpu.roll(both, LANE - odd, 1))

    def spread(j):
        here = columns(j)
        hid_pad[:, here] = pick_columns(hid, 2, j, (head,), tile).astype(BF)
        fac_gate[:, here] = pick_columns(fac_gate_hi, 2, j, (head,), tile) + pick_columns(fac_gate_lo, 2, j, (head,), tile)
        fac_up[:, here] = pick_columns(fac_up_hi, 2, j, (head,), tile) + pick_columns(fac_up_lo, 2, j, (head,), tile)

    def send_result(n):
        out_send[n] = dot(hid_pad[...], weights[:, first + cw * n : first + cw * (n + 1)]).astype(BF)
        send_back(2 + n, out_send.at[n], out_recv.at[n])

    def backward_part(m, n):
        part = dot(grads_in[:, cw * m : cw * (m + 1)], weights[columns(n), first + cw * m : first + cw * (m + 1)], NT)
        if m > 0:
            part = part + hid_grad[:, columns(n)]
        if m < chunks - 1:
            hid_grad[:, columns(n)] = part
        else:
            pg_gate[:, columns(n)] = (part * fac_gate[:, columns(n)]).astype(BF)
            pg_up[:, columns(n)] = (part * fac_up[:, columns(n)]).astype(BF)

    def pack(j, size):
        part = None
        here = slice(size * j, size * (j + 1))
        for row, src in ((3, pg_gate), (4, pg_up)):
            if (table[row, here] >= 0).any():
                more = pick_columns(src, row, j, (), size)
                part = more if part is None else part + more
        pg[:, here] = part.astype(BF)

    tok[width:dp, :] = jnp.zeros((dp - width, toks), BF)
    cot[0:shift, :] = jnp.zeros((shift, toks), BF)
    cot[shift + width : dp, :] = jnp.zeros((dp - shift - width, toks), BF)
    hid[:, width:dp] = jnp.zeros((rows, dp - width), BF)

    pl.semaphore_wait(barrier, len(near))

    count = len(pieces)
    offsets = cfg["offsets"]
    for p in range(count):
        start_swap(p)
    events = []
    for p in range(count):
        events.append((offsets[p] - 1, 0, p, -1))
        events += [(offsets[p] + k, 1, p, k) for k in range(kb)]
        events.append((offsets[p] + kb, 2, p, kb))
    events.sort()
    work = []

    def run(n):
        for _ in range(min(n, len(work))):
            work.pop(0)()

    held = {}

    def prepare_rows():
        held["gate"] = make_slots()
        make_rows()

    def launch_rows():
        send_out(0, rows_send, rows_in)

    def launch_grads():
        make_grads(held["gate"])
        send_out(1, grads_send, grads_in)

    needed = cfg["needed"]
    tiles = dp // tile
    steps = 0
    ended = set()
    round_signal(0)
    for _, _, p, k in events:
        if k == kb and p >= needed:
            run(len(work))
        if k < 0:
            ring_open(p)
        elif k < kb:
            ring_step(p, k)
        else:
            ring_close(p)
            ended.add(p)
        if 0 <= k < kb:
            if steps <= bits:
                round_wait(steps)
                if steps < bits:
                    round_signal(steps + 1)
            if steps == 2:
                prepare_rows()
            if steps == bits + 1:
                launch_rows()
            if steps == bits + 3:
                launch_grads()
            steps += 1
        if k == kb and p == needed - 2:
            for q in range(needed - 1):
                ring_here(q)
            wait_for(rows_in, a2a_recv_sem.at[0])
            work += [functools.partial(forward_main, n) for n in range(head // tile)]
        elif k == kb and p == needed - 1:
            run(len(work))
            ring_here(p)
            work += [forward_rest] + [functools.partial(spread, j) for j in range(tiles)]
            work += [functools.partial(send_result, 0)]
            work += [functools.partial(wait_for, grads_in, a2a_recv_sem.at[1])]
            work += [functools.partial(backward_part, 0, n) for n in range(tiles)]
        elif p >= min(needed - 1, count - 1) and k < kb:
            run(cfg["burst"])
        if k == kb and p >= needed:
            n = p - needed + 1
            ring_here(p)
            send_result(n)
            for m in range(tiles):
                backward_part(n, m)
    for j in range(2 * head // tile):
        pack(j, tile)
    for j in range(2 * head // LANE, pl.cdiv(2 * width, LANE)):
        pack(j, LANE)
    wide = pl.cdiv(2 * width, LANE) * LANE
    for n in range(chunks):
        for m in range(cw // tile):
            here = slice(cw * n + tile * m, cw * n + tile * (m + 1))
            rg_send[n, :, columns(m)] = dot(pg[...], weights[here, 0:wide], NT).astype(BF)
        send_back(2 + chunks + n, rg_send.at[n], rg_recv.at[n])

    eye = onehot(
        lax.broadcasted_iota(jnp.int32, (LANE, LANE), 0) == lax.broadcasted_iota(jnp.int32, (LANE, LANE), 1)
    )
    for n in range(chunks):
        wait_for(out_recv.at[n], a2a_recv_sem.at[2 + n])
        summed = (dot(mix_hi[...], out_recv[n]) + dot(mix_lo[...], out_recv[n])).astype(BF)
        for m in range(cw // LANE):
            d = cw * n + LANE * m - shift
            lo, hi = max(d, 0), min(d + LANE, width)
            if hi > lo:
                turned = dot(eye, summed[:, lanes(m)], NT).astype(BF)
                out_ref[lo:hi, :] = turned[lo - d : hi - d, :]
    turned_tiles = 0
    for n in range(chunks):
        wait_for(rg_recv.at[n], a2a_recv_sem.at[2 + chunks + n])
        rows_nat[:, cw * n : cw * (n + 1)] = dot(pick_t[...], rg_recv[n]).astype(BF)
        for j in range(turned_tiles, pl.cdiv(width, LANE)):
            d = np.arange(LANE * j, min(width, LANE * (j + 1)))
            p = pad * (d // per) + d % per
            start = int(p.min()) // LANE * LANE
            stop = (int(p.max()) // LANE + 1) * LANE
            if stop > cw * (n + 1):
                break
            turned_tiles = j + 1
            di = lax.broadcasted_iota(jnp.int32, (LANE, stop - start), 0) + LANE * j
            sel = onehot(di == table_ref[1:2, start:stop])
            turned = dot(sel, rows_nat[:, start:stop], NT).astype(BF)
            igrad_ref[LANE * j : LANE * j + len(d), :] = turned[0 : len(d), :]

    for p in range(count):
        for way in range(2):
            wait_for(piece(p, 0, kb * pad), ring_send_sem.at[p, way])
        wait_for(piece(p, 0, pad), last_send_sem.at[p])
        wait_for(piece(p, 0, nz * pad), sib_send_sem.at[p])

        @pl.when(swaps)
        def _():
            wait_for(own_piece(p), swap_send.at[p])

    sent(0, rows_send)
    sent(1, grads_send)
    for n in range(chunks):
        sent(2 + n, out_send.at[n])
        sent(2 + chunks + n, rg_send.at[n])


def shards(mesh_shape, tokens, cotangent, expert_ids, gates, gate_up_weight, down_matrix):
    ne = mesh_shape["expert"]
    nz = mesh_shape["fsdp"] // 2
    toks, width = tokens.shape
    per = down_matrix.shape[1]
    pad = pl.cdiv(per, 16) * 16
    cfg = tables(nz, per, pad, width)
    dp, total, head, first = cfg["dp"], cfg["total"], cfg["head"], cfg["first"]
    chunks = 3
    cw = dp // chunks
    tile = 256 if cw % 256 == 0 and head % 256 == 0 else 128
    rows = ne * CAP
    pieces = [(0, head), (head, head), (2 * head, first + cw - 2 * head), (first + cw, cw), (first + 2 * cw, cw)]
    cfg.update(nz=nz, ne=ne, per=per, pad=pad, width=width, tile=tile, pieces=pieces, needed=3, offsets=(0, 0, 1, 3, 3), burst=1)
    any_spec = pl.BlockSpec(memory_space=pl.ANY)
    vmem_spec = pl.BlockSpec(memory_space=pltpu.VMEM)
    dma = pltpu.SemaphoreType.DMA
    flat = (rows, dp)
    wide = pl.cdiv(2 * width, LANE) * LANE
    count = len(pieces)
    out_t, grad_t = pl.pallas_call(
        functools.partial(layer_kernel, cfg),
        out_shape=[pltpu.VMEM((width, toks), BF)] * 2,
        in_specs=[any_spec] * 4 + [vmem_spec] * 3,
        out_specs=[vmem_spec] * 2,
        scratch_shapes=[
            pltpu.VMEM((per, 2 * width), BF),
            pltpu.VMEM((per, width), BF),
            pltpu.VMEM((pad, total), F32),
            pltpu.VMEM((pad, total), BF),
            pltpu.VMEM((dp, total), BF),
            pltpu.VMEM((dp, toks), BF),
            pltpu.VMEM((dp, toks), BF),
            pltpu.VMEM((toks, dp), BF),
        ]
        + [pltpu.VMEM(flat, BF)] * 10
        + [pltpu.VMEM(flat, F32)] * 3
        + [pltpu.VMEM(flat, BF)] * 2
        + [pltpu.VMEM((rows, wide), BF)]
        + [pltpu.VMEM((chunks, rows, cw), BF)] * 4
        + [
            pltpu.VMEM((rows, toks), BF),
            pltpu.VMEM((toks, rows), BF),
            pltpu.VMEM((toks, rows), BF),
            pltpu.VMEM((toks, rows), BF),
            dma((4,)),
            dma((count,)),
            dma((count,)),
            dma((count, 2)),
            dma((count, 2, nz // 2)),
            dma((count,)),
            dma((count,)),
            dma((count,)),
            dma((count,)),
            dma((2 + 2 * chunks,)),
            dma((2 + 2 * chunks,)),
            pltpu.SemaphoreType.REGULAR((ne.bit_length(),)),
        ],
        compiler_params=pltpu.CompilerParams(
            collective_id=0, has_side_effects=True, vmem_limit_bytes=60 * 1024 * 1024
        ),
    )(gate_up_weight[0], down_matrix[0], tokens.T, cotangent.T, expert_ids.T, gates.T, jnp.asarray(cfg["table"]))
    return out_t.T, grad_t.T


def solution(mesh):
    in_specs = (
        P(("fsdp", "expert"), None),
        P(("fsdp", "expert"), None),
        P(("fsdp", "expert"), None),
        P(("fsdp", "expert"), None),
        P("expert", "fsdp", None),
        P("expert", "fsdp", None),
    )
    out_specs = (P(("fsdp", "expert"), None), P(("fsdp", "expert"), None))
    return jax.shard_map(
        functools.partial(shards, dict(mesh.shape)), mesh=mesh, in_specs=in_specs, out_specs=out_specs, check_vma=False
    )
```

```python
import functools

import jax
import jax.numpy as jnp
import numpy as np
from jax import lax
from jax.experimental import pallas as pl
from jax.experimental.pallas import tpu as pltpu
from jax.sharding import PartitionSpec as P

MESH = pl.DeviceIdType.MESH
CAP = 16
LANE = 128
BF = jnp.bfloat16
F32 = jnp.float32
NN = (((1,), (0,)), ((), ()))
NT = (((1,), (1,)), ((), ()))


def dot(a, b, dims=NN):
    return lax.dot_general(a, b, dims, preferred_element_type=F32)


def onehot(mask):
    return jnp.where(mask, 1.0, 0.0).astype(BF)


def windows(idx, width, cuts):
    edges = [0, *cuts, width]
    found = []
    for lo, hi in zip(edges[:-1], edges[1:]):
        part = idx[(idx >= lo) & (idx < hi)]
        if part.size:
            start = int(part.min()) // LANE * LANE
            found.append((start, min(pl.cdiv(int(part.max()) + 1, LANE) * LANE, hi)))
    return found


def tables(nz, per, pad, width):
    ns = 2 * nz
    dp = ns * pad
    main = per // 8 * 8
    rest = per - main
    head = ns * main
    q = np.arange(width)
    s = np.where(q < head, q // main, (q - head) // rest)
    i = np.where(q < head, q % main, main + (q - head) % rest)
    nat_q, pad_q = per * s + i, pad * s + i
    p = np.arange(dp)
    place = np.where(p % pad < per, per * (p // pad) + p % pad, -1)
    packed_p = np.full(dp, -1)
    packed_p[pad_q] = q
    tail = (width - head) // LANE * LANE
    odd = width - head - tail
    gate_q = np.concatenate([np.arange(head), 2 * head + np.arange(tail), 2 * head + 2 * tail + np.arange(odd)])
    up_q = np.concatenate([head + np.arange(head), 2 * head + tail + np.arange(tail), 2 * head + 2 * tail + odd + np.arange(odd)])
    down_at = 2 * width
    total = pl.cdiv(3 * width, LANE) * LANE
    first = down_at // LANE * LANE
    assert total - first == dp and head % LANE == 0
    own = np.full(total, -1)
    own[gate_q] = nat_q
    own[up_q] = width + nat_q
    from_gate = np.full(total, -1)
    from_gate[gate_q] = pad_q
    from_up = np.full(total, -1)
    from_up[up_q] = pad_q
    table = np.full((8, total), -1, np.int32)
    table[0], table[1, :dp], table[2, :dp], table[3], table[4] = own, place, packed_p, from_gate, from_up
    return dict(head=head, tail=tail, odd=odd, first=first, shift=down_at - first, total=total, dp=dp, table=table)


def layer_kernel(
    cfg,
    gate_up_hbm, down_hbm, tok_hbm, cot_hbm, ids_ref, gates_ref, table_ref,
    out_ref, igrad_ref,
    gu_own, dn_own, own32, own, weights,
    tok, cot, rows_nat, rows_send, rows_in, grads_send, grads_in,
    hid, fac_gate_hi, fac_gate_lo, fac_up_hi, fac_up_lo, hid_pad, fac_gate, fac_up, hid_grad, pg_gate, pg_up, pg,
    out_send, rg_send, out_recv, rg_recv,
    pick, pick_t, mix_hi, mix_lo,
    in_sem, swap_send, swap_recv, ring_send_sem, ring_recv_sem, last_send_sem, last_recv_sem,
    sib_send_sem, sib_recv_sem, a2a_send_sem, a2a_recv_sem, round_sem,
):
    nz, ne, per, pad, width = cfg["nz"], cfg["ne"], cfg["per"], cfg["pad"], cfg["width"]
    head, tail, odd, first, shift = cfg["head"], cfg["tail"], cfg["odd"], cfg["first"], cfg["shift"]
    dp, total, table, pieces = cfg["dp"], cfg["total"], cfg["table"], cfg["pieces"]
    chunks, rows, cw = out_send.shape
    tile = cfg["tile"]
    toks = ids_ref.shape[1]
    kb = nz // 2 - 1

    f = lax.axis_index("fsdp")
    e = lax.axis_index("expert")
    ylo = lax.div(f, nz)
    z = lax.rem(f, nz)
    c = lax.rem(e, 2)
    e2 = lax.div(e, 2)
    keeps = ylo == c
    swaps = ylo != c
    znext = ylo * nz + lax.rem(z + 1, nz)
    zprev = ylo * nz + lax.rem(z + nz - 1, nz)

    bits = ne.bit_length() - 1
    partners = [((1 - ylo) * nz + z, e)]
    for r in range(bits):
        bit = lax.rem(lax.div(e, 2**r), 2)
        partners.append((f, e + (1 - 2 * bit) * 2**r))
    swap_partner = ((1 - ylo) * nz + z, e2 * 2 + 1 - c)
    barrier = pltpu.get_barrier_semaphore()
    near = [(znext, e), (zprev, e), swap_partner] + partners
    for there in near:
        pl.semaphore_signal(barrier, inc=1, device_id=there, device_id_type=MESH)

    def round_signal(r):
        pl.semaphore_signal(round_sem.at[r], inc=1, device_id=partners[r], device_id_type=MESH)

    def round_wait(r):
        pl.semaphore_wait(round_sem.at[r], 1)

    load_gu = pltpu.make_async_copy(gate_up_hbm, gu_own, in_sem.at[0])
    load_dn = pltpu.make_async_copy(down_hbm, dn_own, in_sem.at[1])
    load_tok = pltpu.make_async_copy(tok_hbm, tok.at[pl.ds(0, width)], in_sem.at[2])
    load_cot = pltpu.make_async_copy(cot_hbm, cot.at[pl.ds(shift, width)], in_sem.at[3])
    load_gu.start()
    load_dn.start()
    load_tok.start()
    load_cot.start()

    def pick_columns(src, row, j, cuts=(), size=LANE):
        acc = None
        for start, stop in windows(table[row, size * j : size * (j + 1)], src.shape[1], cuts):
            col = lax.broadcasted_iota(jnp.int32, (stop - start, size), 0) + start
            part = dot(src[:, start:stop], onehot(col == table_ref[row : row + 1, size * j : size * (j + 1)]))
            acc = part if acc is None else acc + part
        return acc

    own32[...] = jnp.zeros_like(own32)
    load_gu.wait()
    load_dn.wait()
    for j in range(total // LANE):
        part = None
        if (table[0, LANE * j : LANE * (j + 1)] >= 0).any():
            part = pick_columns(gu_own, 0, j, (width // LANE * LANE,))
        lo = max(LANE * j - 2 * width, 0)
        hi = min(LANE * (j + 1) - 2 * width, width)
        if hi > 0:
            start, stop = lo // LANE * LANE, min(pl.cdiv(hi, LANE) * LANE, width)
            col = lax.broadcasted_iota(jnp.int32, (stop - start, LANE), 0) + (start + 2 * width)
            lane = lax.broadcasted_iota(jnp.int32, (stop - start, LANE), 1) + LANE * j
            more = dot(dn_own[:, start:stop], onehot(col == lane))
            part = more if part is None else part + more
        own32[0:per, LANE * j : LANE * (j + 1)] = part
    own[...] = own32[...].astype(BF)

    def piece(p, at, size):
        start, wide = pieces[p]
        return weights.at[pl.ds(pl.multiple_of(at, 16), size), pl.ds(start, wide)]

    def own_piece(p):
        start, wide = pieces[p]
        return own.at[:, pl.ds(start, wide)]

    def block(p, core, b):
        return piece(p, (core * nz + b) * pad, pad)

    def wait_for(ref, sem):
        pltpu.make_async_copy(ref, ref, sem).wait()

    def start_swap(p):
        @pl.when(keeps)
        def _():
            pltpu.make_async_copy(own_piece(p), block(p, c, z), swap_recv.at[p]).start()

        @pl.when(swaps)
        def _():
            pltpu.make_async_remote_copy(
                src_ref=own_piece(p), dst_ref=block(p, 1 - c, z),
                send_sem=swap_send.at[p], recv_sem=swap_recv.at[p],
                device_id=swap_partner, device_id_type=MESH,
            ).start()

    def ring_send(p, way, k):
        b = lax.rem(z + nz - k, nz) if way == 0 else lax.rem(z + k, nz)
        pltpu.make_async_remote_copy(
            src_ref=block(p, c, b), dst_ref=block(p, c, b),
            send_sem=ring_send_sem.at[p, way], recv_sem=ring_recv_sem.at[p, way, k],
            device_id=(znext if way == 0 else zprev, e), device_id_type=MESH,
        ).start()

    def last_send(p):
        b = lax.rem(z + nz - (1 - 2 * c) * kb, nz)
        pltpu.make_async_remote_copy(
            src_ref=block(p, c, b), dst_ref=block(p, c, b),
            send_sem=last_send_sem.at[p], recv_sem=last_recv_sem.at[p],
            device_id=(ylo * nz + lax.rem(z + nz + 1 - 2 * c, nz), e), device_id_type=MESH,
        ).start()

    def sib_send(p, b):
        pltpu.make_async_remote_copy(
            src_ref=block(p, c, b), dst_ref=block(p, c, b),
            send_sem=sib_send_sem.at[p], recv_sem=sib_recv_sem.at[p],
            device_id=(f, e2 * 2 + 1 - c), device_id_type=MESH,
        ).start()

    def ring_open(p):
        wait_for(block(p, c, z), swap_recv.at[p])
        ring_send(p, 0, 0)
        ring_send(p, 1, 0)
        sib_send(p, z)

    def ring_step(p, k):
        came = (lax.rem(z + nz - 1 - k, nz), lax.rem(z + 1 + k, nz))
        for way in range(2):
            wait_for(block(p, c, came[way]), ring_recv_sem.at[p, way, k])
            if k < kb - 1:
                ring_send(p, way, k + 1)
            sib_send(p, came[way])
        if k == kb - 1:
            last_send(p)

    def ring_close(p):
        b = lax.rem(z + nz // 2, nz)
        wait_for(block(p, c, b), last_recv_sem.at[p])
        sib_send(p, b)

    def ring_here(p):
        wait_for(piece(p, (1 - c) * nz * pad, nz * pad), sib_recv_sem.at[p])

    def far(i, src, dst, gf, ge):
        pltpu.make_async_remote_copy(
            src_ref=src, dst_ref=dst, send_sem=a2a_send_sem.at[i], recv_sem=a2a_recv_sem.at[i],
            device_id=(gf, ge), device_id_type=MESH,
        ).start()

    def same_place(i, src, dst, gf, ge):
        @pl.when(swaps)
        def _():
            far(i, src, dst, gf, ge)

        @pl.when(keeps)
        def _():
            pltpu.make_async_copy(src, dst, a2a_recv_sem.at[i]).start()

    def others(send):
        def one(t, _):
            x = e + jnp.where(t < ne // 2, t + ne // 2, ne - 1 - t)
            send(jnp.where(x >= ne, x - ne, x))
            return 0

        lax.fori_loop(0, ne - 1, one, 0)

    def sixteen(ref, i):
        return ref.at[pl.ds(pl.multiple_of(i * CAP, CAP), CAP)]

    def send_out(i, src, dst):
        def send(x, put=far):
            odd_x = lax.rem(x, 2)
            put(i, sixteen(src, x), sixteen(dst, e), odd_x * nz + z, x - odd_x + ylo)

        others(send)
        send(e, same_place)

    def send_back(i, src, dst):
        def send(x, put=far):
            put(i, sixteen(src, x), sixteen(dst, e2 * 2 + ylo), c * nz + z, x)

        others(send)
        send(e, same_place)

    def sent(i, src):
        @pl.when(keeps)
        def _():
            wait_for(src.at[pl.ds(0, rows - CAP)], a2a_send_sem.at[i])

        @pl.when(swaps)
        def _():
            wait_for(src, a2a_send_sem.at[i])

    def make_slots():
        ci = lax.broadcasted_iota(jnp.int32, (rows, toks), 0)
        expert = lax.shift_right_logical(ci, 4)
        hit = jnp.zeros((rows, toks), F32)
        gate = jnp.zeros((rows, toks), F32)
        for k in range(ids_ref.shape[0]):
            same = ids_ref[k : k + 1, :] == expert
            hit = jnp.where(same, 1.0, hit)
            gate = jnp.where(same, gates_ref[k : k + 1, :], gate)
        earlier = onehot(
            lax.broadcasted_iota(jnp.int32, (toks, toks), 0) < lax.broadcasted_iota(jnp.int32, (toks, toks), 1)
        )
        slot = dot(hit.astype(BF), earlier)
        want = jnp.bitwise_and(ci, CAP - 1).astype(F32)
        kept = jnp.where(slot == want, hit, 0.0)
        gate = gate * kept
        pick[...] = kept.astype(BF)
        pick_t[...] = kept.T.astype(BF)
        mixed = gate.T
        high = mixed.astype(BF)
        mix_hi[...] = high
        mix_lo[...] = (mixed - high.astype(F32)).astype(BF)
        return jnp.sum(gate, axis=1, keepdims=True)

    def columns(n, base=0):
        return slice(base + tile * n, base + tile * (n + 1))

    def lanes(j):
        return slice(LANE * j, LANE * (j + 1))

    def make_rows():
        load_tok.wait()
        for n in range(dp // tile):
            rows_nat[:, columns(n)] = dot(pick[...], tok[columns(n), :], NT).astype(BF)
        for j in range(dp // LANE):
            rows_send[:, lanes(j)] = pick_columns(rows_nat, 1, j).astype(BF)

    def make_grads(slot_gate):
        load_cot.wait()
        for n in range(dp // tile):
            grads_send[:, columns(n)] = (dot(pick[...], cot[columns(n), :], NT) * slot_gate).astype(BF)

    def activate(at, act, upper):
        here = slice(at, at + act.shape[1])
        sigma = jax.nn.sigmoid(act)
        gated = act * sigma
        hid[:, here] = (gated * upper).astype(BF)
        slope = upper * sigma * (1.0 + act * (1.0 - sigma))
        for value, high_ref, low_ref in ((slope, fac_gate_hi, fac_gate_lo), (gated, fac_up_hi, fac_up_lo)):
            high = value.astype(BF)
            high_ref[:, here] = high
            low_ref[:, here] = (value - high.astype(F32)).astype(BF)

    def forward_main(n):
        activate(
            tile * n, dot(rows_in[...], weights[:, columns(n)]), dot(rows_in[...], weights[:, columns(n, head)])
        )

    def forward_rest():
        at = 2 * head
        if tail:
            both = dot(rows_in[...], weights[:, at : at + 2 * tail])
            activate(head, both[:, 0:tail], both[:, tail : 2 * tail])
        both = dot(rows_in[...], weights[:, at + 2 * tail : at + 2 * tail + LANE])
        activate(head + tail, both, pltpu.roll(both, LANE - odd, 1))

    def spread(j):
        here = columns(j)
        hid_pad[:, here] = pick_columns(hid, 2, j, (head,), tile).astype(BF)
        fac_gate[:, here] = pick_columns(fac_gate_hi, 2, j, (head,), tile) + pick_columns(fac_gate_lo, 2, j, (head,), tile)
        fac_up[:, here] = pick_columns(fac_up_hi, 2, j, (head,), tile) + pick_columns(fac_up_lo, 2, j, (head,), tile)

    def send_result(n):
        out_send[n] = dot(hid_pad[...], weights[:, first + cw * n : first + cw * (n + 1)]).astype(BF)
        send_back(2 + n, out_send.at[n], out_recv.at[n])

    def backward_part(m, n):
        part = dot(grads_in[:, cw * m : cw * (m + 1)], weights[columns(n), first + cw * m : first + cw * (m + 1)], NT)
        if m > 0:
            part = part + hid_grad[:, columns(n)]
        if m < chunks - 1:
            hid_grad[:, columns(n)] = part
        else:
            pg_gate[:, columns(n)] = (part * fac_gate[:, columns(n)]).astype(BF)
            pg_up[:, columns(n)] = (part * fac_up[:, columns(n)]).astype(BF)

    def pack(j, size):
        part = None
        here = slice(size * j, size * (j + 1))
        for row, src in ((3, pg_gate), (4, pg_up)):
            if (table[row, here] >= 0).any():
                more = pick_columns(src, row, j, (), size)
                part = more if part is None else part + more
        pg[:, here] = part.astype(BF)

    tok[width:dp, :] = jnp.zeros((dp - width, toks), BF)
    cot[0:shift, :] = jnp.zeros((shift, toks), BF)
    cot[shift + width : dp, :] = jnp.zeros((dp - shift - width, toks), BF)
    hid[:, width:dp] = jnp.zeros((rows, dp - width), BF)

    pl.semaphore_wait(barrier, len(near))

    count = len(pieces)
    offsets = cfg["offsets"]
    for p in range(count):
        start_swap(p)
    events = []
    for p in range(count):
        events.append((offsets[p] - 1, 0, p, -1))
        events += [(offsets[p] + k, 1, p, k) for k in range(kb)]
        events.append((offsets[p] + kb, 2, p, kb))
    events.sort()
    work = []

    def run(n):
        for _ in range(min(n, len(work))):
            work.pop(0)()

    held = {}

    def prepare_rows():
        held["gate"] = make_slots()
        make_rows()

    def launch_rows():
        send_out(0, rows_send, rows_in)

    def launch_grads():
        make_grads(held["gate"])
        send_out(1, grads_send, grads_in)

    needed = cfg["needed"]
    tiles = dp // tile
    steps = 0
    ended = set()
    late = []
    round_signal(0)
    for _, _, p, k in events:
        if k == kb and p >= needed:
            run(len(work))
        if k < 0:
            ring_open(p)
        elif k < kb:
            ring_step(p, k)
        else:
            ring_close(p)
            ended.add(p)
            while late:
                late.pop(0)()
        if 0 <= k < kb:
            if steps <= bits:
                round_wait(steps)
                if steps < bits:
                    round_signal(steps + 1)
            if steps == 2:
                prepare_rows()
            if steps == bits + 1:
                launch_rows()
            if steps == bits + 3:
                launch_grads()
            steps += 1
        if k == kb and p == needed - 2:
            for q in range(needed - 1):
                ring_here(q)
            wait_for(rows_in, a2a_recv_sem.at[0])
            work += [functools.partial(forward_main, n) for n in range(head // tile)]
        elif k == kb and p == needed - 1:
            run(len(work))
            ring_here(p)
            work += [forward_rest] + [functools.partial(spread, j) for j in range(tiles)]
            work += [functools.partial(send_result, 0)]
            work += [functools.partial(wait_for, grads_in, a2a_recv_sem.at[1])]
            work += [functools.partial(backward_part, 0, n) for n in range(tiles)]
        elif p >= min(needed - 1, count - 1) and k < kb:
            run(cfg["burst"])
        if k == kb and p >= needed:
            n = p - needed + 1
            ring_here(p)
            send_result(n)
            for m in range(tiles):
                if n < chunks - 1:
                    late.append(functools.partial(backward_part, n, m))
                else:
                    backward_part(n, m)
    for j in range(2 * head // tile):
        pack(j, tile)
    for j in range(2 * head // LANE, pl.cdiv(2 * width, LANE)):
        pack(j, LANE)
    wide = pl.cdiv(2 * width, LANE) * LANE
    for n in range(chunks):
        for m in range(cw // tile):
            here = slice(cw * n + tile * m, cw * n + tile * (m + 1))
            rg_send[n, :, columns(m)] = dot(pg[...], weights[here, 0:wide], NT).astype(BF)
        send_back(2 + chunks + n, rg_send.at[n], rg_recv.at[n])

    eye = onehot(
        lax.broadcasted_iota(jnp.int32, (LANE, LANE), 0) == lax.broadcasted_iota(jnp.int32, (LANE, LANE), 1)
    )
    for n in range(chunks):
        wait_for(out_recv.at[n], a2a_recv_sem.at[2 + n])
        summed = (dot(mix_hi[...], out_recv[n]) + dot(mix_lo[...], out_recv[n])).astype(BF)
        for m in range(cw // LANE):
            d = cw * n + LANE * m - shift
            lo, hi = max(d, 0), min(d + LANE, width)
            if hi > lo:
                turned = dot(eye, summed[:, lanes(m)], NT).astype(BF)
                out_ref[lo:hi, :] = turned[lo - d : hi - d, :]
    turned_tiles = 0
    for n in range(chunks):
        wait_for(rg_recv.at[n], a2a_recv_sem.at[2 + chunks + n])
        rows_nat[:, cw * n : cw * (n + 1)] = dot(pick_t[...], rg_recv[n]).astype(BF)
        for j in range(turned_tiles, pl.cdiv(width, LANE)):
            d = np.arange(LANE * j, min(width, LANE * (j + 1)))
            p = pad * (d // per) + d % per
            start = int(p.min()) // LANE * LANE
            stop = (int(p.max()) // LANE + 1) * LANE
            if stop > cw * (n + 1):
                break
            turned_tiles = j + 1
            di = lax.broadcasted_iota(jnp.int32, (LANE, stop - start), 0) + LANE * j
            sel = onehot(di == table_ref[1:2, start:stop])
            turned = dot(sel, rows_nat[:, start:stop], NT).astype(BF)
            igrad_ref[LANE * j : LANE * j + len(d), :] = turned[0 : len(d), :]

    for p in range(count):
        for way in range(2):
            wait_for(piece(p, 0, kb * pad), ring_send_sem.at[p, way])
        wait_for(piece(p, 0, pad), last_send_sem.at[p])
        wait_for(piece(p, 0, nz * pad), sib_send_sem.at[p])

        @pl.when(swaps)
        def _():
            wait_for(own_piece(p), swap_send.at[p])

    sent(0, rows_send)
    sent(1, grads_send)
    for n in range(chunks):
        sent(2 + n, out_send.at[n])
        sent(2 + chunks + n, rg_send.at[n])


def shards(mesh_shape, tokens, cotangent, expert_ids, gates, gate_up_weight, down_matrix):
    ne = mesh_shape["expert"]
    nz = mesh_shape["fsdp"] // 2
    toks, width = tokens.shape
    per = down_matrix.shape[1]
    pad = pl.cdiv(per, 16) * 16
    cfg = tables(nz, per, pad, width)
    dp, total, head, first = cfg["dp"], cfg["total"], cfg["head"], cfg["first"]
    chunks = 3
    cw = dp // chunks
    tile = 256 if cw % 256 == 0 and head % 256 == 0 else 128
    rows = ne * CAP
    pieces = [(0, head), (head, head), (2 * head, first + cw - 2 * head), (first + cw, cw), (first + 2 * cw, cw)]
    cfg.update(nz=nz, ne=ne, per=per, pad=pad, width=width, tile=tile, pieces=pieces, needed=3, offsets=(0, 0, 1, 3, 3), burst=1)
    any_spec = pl.BlockSpec(memory_space=pl.ANY)
    vmem_spec = pl.BlockSpec(memory_space=pltpu.VMEM)
    dma = pltpu.SemaphoreType.DMA
    flat = (rows, dp)
    wide = pl.cdiv(2 * width, LANE) * LANE
    count = len(pieces)
    out_t, grad_t = pl.pallas_call(
        functools.partial(layer_kernel, cfg),
        out_shape=[pltpu.VMEM((width, toks), BF)] * 2,
        in_specs=[any_spec] * 4 + [vmem_spec] * 3,
        out_specs=[vmem_spec] * 2,
        scratch_shapes=[
            pltpu.VMEM((per, 2 * width), BF),
            pltpu.VMEM((per, width), BF),
            pltpu.VMEM((pad, total), F32),
            pltpu.VMEM((pad, total), BF),
            pltpu.VMEM((dp, total), BF),
            pltpu.VMEM((dp, toks), BF),
            pltpu.VMEM((dp, toks), BF),
            pltpu.VMEM((toks, dp), BF),
        ]
        + [pltpu.VMEM(flat, BF)] * 10
        + [pltpu.VMEM(flat, F32)] * 3
        + [pltpu.VMEM(flat, BF)] * 2
        + [pltpu.VMEM((rows, wide), BF)]
        + [pltpu.VMEM((chunks, rows, cw), BF)] * 4
        + [
            pltpu.VMEM((rows, toks), BF),
            pltpu.VMEM((toks, rows), BF),
            pltpu.VMEM((toks, rows), BF),
            pltpu.VMEM((toks, rows), BF),
            dma((4,)),
            dma((count,)),
            dma((count,)),
            dma((count, 2)),
            dma((count, 2, nz // 2)),
            dma((count,)),
            dma((count,)),
            dma((count,)),
            dma((count,)),
            dma((2 + 2 * chunks,)),
            dma((2 + 2 * chunks,)),
            pltpu.SemaphoreType.REGULAR((ne.bit_length(),)),
        ],
        compiler_params=pltpu.CompilerParams(
            collective_id=0, has_side_effects=True, vmem_limit_bytes=60 * 1024 * 1024
        ),
    )(gate_up_weight[0], down_matrix[0], tokens.T, cotangent.T, expert_ids.T, gates.T, jnp.asarray(cfg["table"]))
    return out_t.T, grad_t.T


def solution(mesh):
    in_specs = (
        P(("fsdp", "expert"), None),
        P(("fsdp", "expert"), None),
        P(("fsdp", "expert"), None),
        P(("fsdp", "expert"), None),
        P("expert", "fsdp", None),
        P("expert", "fsdp", None),
    )
    out_specs = (P(("fsdp", "expert"), None), P(("fsdp", "expert"), None))
    return jax.shard_map(
        functools.partial(shards, dict(mesh.shape)), mesh=mesh, in_specs=in_specs, out_specs=out_specs, check_vma=False
    )
```
